32 devices in a mesh: groups: 2 (over y), fsdp: 8 (over z, core), band: 2 (over x).
Axes of the slice: x: 2, y: 2, z: 4, core: 2. Of those that a mesh axis runs over, the one named last changes fastest.
Arguments:
- hidden_in: bfloat16 [16, 4, 64, 5632], P(('groups', 'fsdp'), 'band'), parts along dimension 0, may hold values from -6 to 6
- tap_weights: bfloat16 [9, 5632], P(None, 'fsdp'), may hold values from -2 to 2
- tap_bias: bfloat16 [5632], P('fsdp'), may hold values from -3 to 3
- w_out: bfloat16 [2816, 2240], P('fsdp'), may hold values from -0.109375 to 0.109375
- cotangent: bfloat16 [16, 4, 64, 2240], P(('groups', 'fsdp'), 'band'), parts along dimension 0, may hold values from -0.59765625 to 0.59765625
Outputs:
- block_out: bfloat16 [16, 4, 64, 2240], P(('groups', 'fsdp'), 'band'), parts along dimension 0
- d_hidden: bfloat16 [16, 4, 64, 5632], P(('groups', 'fsdp'), 'band'), parts along dimension 0
- d_taps: float32 [18, 5632], P('groups', 'fsdp'), parts along dimension 0
- d_tap_bias: float32 [11264], P(('groups', 'fsdp')), parts along dimension 0
The draws below stay inside these ranges and needn't reach their ends.
There are 2 independent parts, one for each index of `groups`. The reference program is written for one: setup_inputs(seed, part) draws one part's arguments, and reference() takes and returns one part's arrays. A program takes and returns all parts, laid end to end along the dimension named above; an argument that names none is the same for every part. Nothing has to cross between parts.
All inputs are finite; a program needn't handle non-finite values.
Results may differ from the reference program's by a relative error of at most 0.0049.
Values may be sent and summed in bfloat16 or wider, within the bound.
No kernel may reach another device: no remote copies, remote signals or barrier semaphores. Data moves between devices by JAX's collectives and lax.ppermute only.
A program may use at most 128 MiB of HBM per device.

```python
import jax
import jax.numpy as jnp
from jax import lax

D = 2240
HID = 2816
CH = 5632
COLS = 64
ROWS = 4
SAMPLES = 8


def shard_levels(own_key, extent, pieces, low, largest):
    def one(axis_at, shards_of):
        draws = jax.random.uniform(jax.random.fold_in(jax.random.fold_in(own_key, 6), axis_at), (shards_of,), jnp.float32, low / len(pieces), largest / len(pieces))
        return jnp.repeat(jnp.exp(draws), extent[axis_at] // shards_of).reshape((-1,) + (1,) * (len(extent) - axis_at - 1))

    level = one(*pieces[0])
    for cut in pieces[1:]:
        level = level * one(*cut)
    return level


def centred(own_key, dims, width, most, cuts=(), held_as=jnp.bfloat16):
    array = jax.random.normal(own_key, dims, jnp.float32) * width
    if len(cuts) > 0:
        array = shard_levels(own_key, dims, cuts, -0.22, 0.18) * array
    return jnp.clip(array, min=-most, max=most).astype(held_as)


def setup_inputs(seed: int = 0, part: int = 0) -> dict:
    keys = jax.random.split(jax.random.key(seed), 6)
    part_keys = jax.random.split(jax.random.fold_in(keys[5], part), 6)
    hidden_in = centred(part_keys[0], (SAMPLES, ROWS, COLS, CH), 1.0, 6.0, ((0, 8), (1, 2)))
    tap_weights = centred(keys[1], (9, CH), 9 ** -0.5, 2.0, ((1, 8),))
    tap_bias = centred(keys[2], (CH,), 0.5, 3.0, ((0, 8),))
    w_out = centred(keys[3], (HID, D), HID ** -0.5, 0.109375, ((0, 8),))
    cotangent = centred(part_keys[4], (SAMPLES, ROWS, COLS, D), 0.1, 0.59765625, ((0, 8), (1, 2)))
    return {"hidden_in": hidden_in, "tap_weights": tap_weights, "tap_bias": tap_bias, "w_out": w_out, "cotangent": cotangent}


def one_image(pair, tap_weights, tap_bias, w_out):
    image, grad_out = pair
    row_count, col_count, channels = image.shape
    hidden_units = channels // 2
    padded = jnp.pad(image, ((1, 1), (1, 1), (0, 0)))
    kernel = tap_weights.astype(jnp.float32)
    offset = tap_bias.astype(jnp.float32)
    summed = jnp.zeros((row_count, col_count, channels), jnp.float32) + offset
    for tap_row in range(3):
        for tap_col in range(3):
            window = padded[tap_row:tap_row + row_count, tap_col:tap_col + col_count, :].astype(jnp.float32)
            summed = summed + kernel[3 * tap_row + tap_col] * window
    values_half = summed[..., :hidden_units]
    gate_half = summed[..., hidden_units:]
    sigmoid_gate = jax.nn.sigmoid(gate_half)
    silu_gate = gate_half * sigmoid_gate
    glu_out = (values_half * silu_gate).astype(jnp.bfloat16)
    flat_glu = glu_out.reshape(row_count * col_count, hidden_units)
    block_out = jnp.dot(flat_glu, w_out, preferred_element_type=jnp.float32).astype(jnp.bfloat16)
    block_out = block_out.reshape(row_count, col_count, -1)
    flat_grad = grad_out.reshape(row_count * col_count, -1)
    d_glu = jnp.dot(flat_grad, w_out.T, preferred_element_type=jnp.float32).reshape(row_count, col_count, hidden_units)
    slope = sigmoid_gate * (1.0 + gate_half * (1.0 - sigmoid_gate))
    d_pre = jnp.concatenate([d_glu * silu_gate, d_glu * values_half * slope], axis=-1).astype(jnp.bfloat16)
    d_pad = jnp.pad(d_pre, ((1, 1), (1, 1), (0, 0))).astype(jnp.float32)
    d_pre_wide = d_pre.astype(jnp.float32)
    d_image = jnp.zeros((row_count, col_count, channels), jnp.float32)
    tap_terms = []
    for tap_row in range(3):
        for tap_col in range(3):
            d_image = d_image + kernel[3 * tap_row + tap_col] * d_pad[2 - tap_row:2 - tap_row + row_count, 2 - tap_col:2 - tap_col + col_count, :]
            window = padded[tap_row:tap_row + row_count, tap_col:tap_col + col_count, :].astype(jnp.float32)
            tap_terms.append(jnp.sum(window * d_pre_wide, axis=(0, 1)))
    return block_out, d_image.astype(jnp.bfloat16), jnp.stack(tap_terms), jnp.sum(d_pre_wide, axis=(0, 1))


def reference(hidden_in, tap_weights, tap_bias, w_out, cotangent):
    def apply_one(pair):
        return one_image(pair, tap_weights, tap_bias, w_out)

    block_out, d_hidden, tap_parts, bias_parts = lax.map(apply_one, (hidden_in, cotangent))
    return block_out, d_hidden, jnp.sum(tap_parts, axis=0), jnp.sum(bias_parts, axis=0)
```

```python
import functools

import jax
import jax.numpy as jnp
from jax import lax
from jax.experimental import pallas as pl
from jax.experimental.pallas import tpu as pltpu
from jax.sharding import PartitionSpec as P

F32 = jnp.float32
BF16 = jnp.bfloat16
LANES = 128


def up(value, step):
    return -(-value // step) * step


def pack_kernel(n, jb, blk, s_ref, x_ref, *outs):
    b = s_ref[0]
    tokens = x_ref.shape[0]
    rows, cols = outs[0].shape[2:4]
    chans = x_ref.shape[1]
    for vg in range(2):
        for jz in range(jb):
            for t in range(n):
                start = ((vg * jb + jz) * n + t) * blk
                low = start // LANES * LANES
                high = min(up(start + blk, LANES), chans)
                wide = x_ref[:, low:high].astype(F32)
                if start != low:
                    wide = pltpu.roll(wide, high - low - (start - low), 1)
                piece = wide[:, :blk].astype(BF16).reshape(rows, cols, blk)
                for k in range(n):

                    @pl.when(lax.rem(b + k, n) == t)
                    def _():
                        outs[k][vg, jz] = piece


def place_rows(n, rl, b, xs, own, received):
    for vg in range(2):
        for i in range(rl):
            xs[vg, b * rl + i] = own[vg, 0, i].astype(F32)
            for k in range(1, n):
                src = lax.rem(b - k + n, n)
                xs[vg, src * rl + i] = received[k - 1][vg, 0, i].astype(F32)


def shifted(row):
    cols = row.shape[0]
    at = lax.broadcasted_iota(jnp.int32, row.shape, 0)
    prev = jnp.where(at == 0, 0.0, pltpu.roll(row, 1, 0))
    nxt = jnp.where(at == cols - 1, 0.0, pltpu.roll(row, cols - 1, 0))
    return prev, row, nxt


def conv_kernel(n, jb, rl, s_ref, own, *refs):
    received, (taps, glu, silu, slope, xs) = refs[: n - 1], refs[n - 1 :]
    b, tap_mask = s_ref[0], s_ref[1]
    jz = pl.program_id(0)
    place_rows(n, rl, b, xs, own, received)
    total = n * rl
    pre = []
    for vg in range(2):
        w = taps[(vg * jb + jz) ^ tap_mask].astype(F32)
        acc = [None] * total
        for r in range(total):
            parts = shifted(xs[vg, r])
            for i in range(3):
                to = r + 1 - i
                if 0 <= to < total:
                    for j in range(3):
                        term = w[3 * i + j : 3 * i + j + 1] * parts[j]
                        acc[to] = term if acc[to] is None else acc[to] + term
        pre.append([a + w[9:10] for a in acc])
    for r in range(total):
        rel = lax.rem(r // rl - b + n, n)
        values, gate = pre[0][r], pre[1][r]
        sigma = jax.nn.sigmoid(gate)
        act = gate * sigma
        cols = values.shape[0]
        spot = pl.ds(r % rl * cols, cols)
        glu[0, rel, spot, :] = (values * act).astype(BF16)
        silu[0, rel, spot, :] = act
        slope[0, rel, spot, :] = values * (sigma * (1.0 + gate * (1.0 - sigma)))


def load_weights(s_ref, copies, w_refs, w_buf, sems):
    own_core = s_ref[2]
    waits = []
    for k, (main, other) in enumerate(copies):
        def run(options, action, k=k):
            for src, slot in options:
                where = w_buf.at[k] if slot is None else w_buf.at[k, slot]
                getattr(pltpu.make_async_copy(src, where, sems.at[k]), action)()

        def both(action, main=main, other=other, run=run):
            if other is None:
                run(main(s_ref, w_refs), action)
                return
            @pl.when(own_core == 1)
            def _():
                run(main(s_ref, w_refs), action)

            @pl.when(own_core == 0)
            def _():
                run(other(s_ref, w_refs), action)

        both("start")
        waits.append(functools.partial(both, "wait"))
    return waits


def out_kernel(n, jb, copies, n_w, s_ref, glu, *refs):
    w_refs, outs, (w_buf, acc, sems) = refs[:n_w], refs[n_w : n_w + n], refs[n_w + n :]
    waits = load_weights(s_ref, copies, w_refs, w_buf, sems)
    tokens = glu.shape[2]
    for k in range(len(copies)):
        waits[k]()
        jz = s_ref[3] ^ k
        part = jnp.dot(
            glu[jz].reshape(n * tokens, glu.shape[3]),
            w_buf[k].reshape(glu.shape[3], w_buf.shape[3]),
            preferred_element_type=F32,
        )
        if k == 0:
            acc[...] = part
        else:
            acc[...] += part
    for k in range(n):
        outs[k][...] = acc[k * tokens : (k + 1) * tokens, :].astype(outs[k].dtype)


def grad_kernel(n, jb, rl, copies, n_w, s_ref, own, *refs):
    received = refs[: n - 1]
    taps, silu, slope = refs[n - 1 : n + 2]
    cots = refs[n + 2 : 2 * n + 2]
    w_refs = refs[2 * n + 2 : 2 * n + 2 + n_w]
    rest = refs[2 * n + 2 + n_w :]
    outs, (tap_grad, xs, dp, dh, w_buf, sems) = rest[:n], rest[n:]
    b, tap_mask = s_ref[0], s_ref[1]
    step = pl.program_id(0)
    jz = s_ref[3] ^ step

    @pl.when(step == 0)
    def _():
        load_weights(s_ref, copies, w_refs, w_buf, sems)

    for k in range(len(copies)):
        @pl.when(step == k)
        def _():
            wait_weights(s_ref, copies, w_refs, w_buf, sems, k)

    place_rows(n, rl, b, xs, own, received)
    total = n * rl
    tokens, blk = silu.shape[2:]
    cols = tokens // rl
    w_now = w_buf[step].reshape(blk, w_buf.shape[3])
    for k in range(n):
        d_glu = lax.dot_general(
            cots[k][...], w_now, (((1,), (1,)), ((), ())), preferred_element_type=F32
        )
        dp[0, k] = (d_glu * silu[0, k]).astype(BF16).astype(F32).reshape(rl, cols, blk)
        dp[1, k] = (d_glu * slope[0, k]).astype(BF16).astype(F32).reshape(rl, cols, blk)
    for vg in range(2):
        w = taps[(vg * jb + jz) ^ tap_mask].astype(F32)
        acc = [None] * total
        sums = [None] * 10
        for r in range(total):
            rel = lax.rem(r // rl - b + n, n)
            row = dp[vg, rel, r % rl]
            nxt_prev = shifted(row)
            sums[9] = row if sums[9] is None else sums[9] + row
            for i in range(3):
                to = r - 1 + i
                if 0 <= to < total:
                    x = xs[vg, to]
                    for j in range(3):
                        seen = nxt_prev[2 - j]
                        tap = 3 * i + j
                        term = w[tap : tap + 1] * seen
                        acc[to] = term if acc[to] is None else acc[to] + term
                        prod = x * seen
                        sums[tap] = prod if sums[tap] is None else sums[tap] + prod
        for r in range(total):
            rel = lax.rem(r // rl - b + n, n)
            dh[rel, vg, r % rl] = acc[r].astype(BF16)
        tap_grad[vg, 0, :10, :] = jnp.concatenate(
            [jnp.sum(s, axis=0, keepdims=True) for s in sums], axis=0
        )
    for k in range(n):
        for vg in range(2):
            outs[k][vg, 0] = dh[k, vg]


def wait_weights(s_ref, copies, w_refs, w_buf, sems, k):
    main, other = copies[k]

    def run(options):
        for src, slot in options:
            where = w_buf.at[k] if slot is None else w_buf.at[k, slot]
            pltpu.make_async_copy(src, where, sems.at[k]).wait()

    if other is None:
        run(main(s_ref, w_refs))
        return

    @pl.when(s_ref[2] == 1)
    def _():
        run(main(s_ref, w_refs))

    @pl.when(s_ref[2] == 0)
    def _():
        run(other(s_ref, w_refs))


def unpack_kernel(n, jb, blk, s_ref, *refs):
    ins, out, (held,) = refs[:n], refs[n], refs[n + 1 :]
    b = s_ref[0]
    rl, cols = ins[0].shape[2:4]
    for k in range(n):
        held[lax.rem(b - k + n, n)] = ins[k][...]
    for vg in range(2):
        for jz in range(jb):
            for t in range(n):
                start = ((vg * jb + jz) * n + t) * blk
                out[:, start : start + blk] = held[t, vg, jz].reshape(rl * cols, blk)


def body(hidden_in, tap_weights, tap_bias, w_out, cotangent):
    groups, shards, n = (lax.axis_size(a) for a in ("groups", "fsdp", "band"))
    images, rl, cols, chans = hidden_in.shape
    hidden = chans // 2
    blk = w_out.shape[0]
    jb = shards // n
    feats = w_out.shape[1]
    tokens = rl * cols
    g, f, b = (lax.axis_index(a) for a in ("groups", "fsdp", "band"))
    fast = n == 2 and groups == 2 and shards % 4 == 0 and shards & (shards - 1) == 0 and blk % 32 == 0
    assert images == 1 and shards % n == 0

    tap_block = jnp.concatenate(
        [tap_weights, tap_bias[None], jnp.zeros((6, tap_bias.shape[0]), BF16)], axis=0
    )
    if fast:
        scalars = jnp.stack([b, f, jnp.where(f % 2 == b, 1, 0), f // n, g]).astype(jnp.int32)
    else:
        scalars = jnp.stack([b, 0 * f, 0 * f + 1, 0 * f, g]).astype(jnp.int32)

    if fast:
        every = ("groups", "fsdp", "band")
        zr = jb

        def across(x, flip, name):
            pairs = [(s * n + t, (s ^ flip) * n + t) for s in range(shards) for t in range(n) if s % 2 == t]
            with jax.named_scope(name):
                return lax.ppermute(x, ("fsdp", "band"), pairs)

        def other_group(x, name):
            size = shards * n
            pairs = [
                (p * size + s * n + t, (1 - p) * size + s * n + t)
                for p in range(2) for s in range(shards) for t in range(n) if s % 2 == t
            ]
            with jax.named_scope(name):
                return lax.ppermute(x, every, pairs)

        half = lax.dynamic_slice_in_dim(w_out, g * (blk // 2), blk // 2, 0)
        mine = {0: half}
        flips = 1
        order = []
        bit = zr // 2
        while bit:
            order.append(bit)
            bit //= 2
        for bit in order:
            for k in list(mine):
                mine[k ^ bit] = across(mine[k], 2 * bit, f"wz{k ^ bit}")
        w_args, copies = [], []
        for k in range(zr):
            base = len(w_args)
            if k == 0:
                whole = w_out.reshape(2, blk // 2, feats)
                w_args += [whole, across(w_out, 1, "wc0").reshape(2, blk // 2, feats)]
                copies.append((
                    lambda s, w, i=base: [(w[i], None)],
                    lambda s, w, i=base + 1: [(w[i], None)],
                ))
            else:
                a, y = mine[k], other_group(mine[k], f"wy{k}")
                w_args += [a, y, across(a, 1, f"wca{k}"), across(y, 1, f"wcy{k}")]
                copies.append((
                    lambda s, w, i=base: [(w[i], s[4]), (w[i + 1], 1 - s[4])],
                    lambda s, w, i=base + 2: [(w[i], s[4]), (w[i + 1], 1 - s[4])],
                ))
        parts = 2
    else:
        w_all = lax.all_gather(w_out, "fsdp", axis=0, tiled=True).reshape(jb, n, 1, blk, feats)
        w_args = [lax.dynamic_index_in_dim(w_all, b, 1, keepdims=False)]
        copies = [(lambda s, w, k=k: [(w[0].at[k], None)], None) for k in range(jb)]
        parts = 1

    if fast:
        tap_all = lax.dynamic_slice_in_dim(tap_block, b * blk, blk, 1)[None]
        step = 1
        while step < shards:
            with jax.named_scope(f"tap{step}"):
                other = lax.ppermute(tap_all, "fsdp", [(i, i ^ step) for i in range(shards)])
            tap_all = jnp.concatenate([tap_all, other], axis=0)
            step *= 2
    else:
        tap_all = lax.all_gather(tap_block, "fsdp", axis=1, tiled=True)
        tap_all = tap_all.reshape(16, 2 * jb, n, blk)
        tap_all = lax.dynamic_index_in_dim(tap_all, b, 2, keepdims=False).transpose(1, 0, 2)

    vmem = pl.BlockSpec(memory_space=pltpu.VMEM)
    smem = pl.BlockSpec(memory_space=pltpu.SMEM)
    part_shape = (2, jb, rl, cols, blk)
    packed = pl.pallas_call(
        functools.partial(pack_kernel, n, jb, blk),
        out_shape=[jax.ShapeDtypeStruct(part_shape, BF16)] * n,
        in_specs=[smem, vmem],
        out_specs=[vmem] * n,
        name="pack",
    )(scalars, hidden_in.reshape(tokens, chans))
    def turn(x, k, name):
        with jax.named_scope(name):
            return lax.ppermute(x, "band", [(i, (i + k) % n) for i in range(n)])
    hid_in = [turn(packed[k], k, f"hid{k}") for k in range(1, n)]
    cot = cotangent.reshape(tokens, feats)
    cots = [cot] + [turn(cot, n - k, f"cot{k}") for k in range(1, n)]

    part_spec = pl.BlockSpec((2, 1, rl, cols, blk), lambda j, s: (0, j, 0, 0, 0))
    tap_spec = pl.BlockSpec((2 * jb, 16, blk), lambda j, s: (0, 0, 0))
    act_spec = pl.BlockSpec((1, n, tokens, blk), lambda j, s: (j, 0, 0, 0))
    act_shape = (jb, n, tokens, blk)
    glu, silu, slope = pl.pallas_call(
        functools.partial(conv_kernel, n, jb, rl),
        grid_spec=pltpu.PrefetchScalarGridSpec(
            num_scalar_prefetch=1,
            grid=(jb,),
            in_specs=[part_spec] * n + [tap_spec],
            out_specs=[act_spec] * 3,
            scratch_shapes=[pltpu.VMEM((2, n * rl, cols, blk), F32)],
        ),
        out_shape=[
            jax.ShapeDtypeStruct(act_shape, BF16),
            jax.ShapeDtypeStruct(act_shape, F32),
            jax.ShapeDtypeStruct(act_shape, F32),
        ],
        name="conv",
    )(scalars, packed[0], *hid_in, tap_all)

    any_spec = pl.BlockSpec(memory_space=pl.ANY)
    w_scratch = pltpu.VMEM((jb, parts, blk // parts, feats), BF16)
    partial_out = pl.pallas_call(
        functools.partial(out_kernel, n, jb, copies, len(w_args)),
        in_specs=[smem, vmem] + [any_spec] * len(w_args),
        out_specs=[vmem] * n,
        out_shape=[jax.ShapeDtypeStruct((tokens, feats), F32 if k == 0 else BF16) for k in range(n)],
        scratch_shapes=[w_scratch, pltpu.VMEM((n * tokens, feats), F32), pltpu.SemaphoreType.DMA((jb,))],
        name="project",
    )(scalars, glu, *w_args)
    block_out = partial_out[0]
    for k in range(1, n):
        block_out = block_out + turn(partial_out[k], k, f"bo{k}").astype(F32)
    block_out = block_out.astype(BF16)

    part_at = pl.BlockSpec((2, 1, rl, cols, blk), lambda j, s: (0, s[3] ^ j, 0, 0, 0))
    act_at = pl.BlockSpec((1, n, tokens, blk), lambda j, s: (s[3] ^ j, 0, 0, 0))
    cot_spec = pl.BlockSpec((tokens, feats), lambda j, s: (0, 0))
    grads = pl.pallas_call(
        functools.partial(grad_kernel, n, jb, rl, copies, len(w_args)),
        grid_spec=pltpu.PrefetchScalarGridSpec(
            num_scalar_prefetch=1,
            grid=(jb,),
            in_specs=[part_at] * n + [tap_spec, act_at, act_at] + [cot_spec] * n + [any_spec] * len(w_args),
            out_specs=[part_at] * n + [pl.BlockSpec((2, 1, 16, blk), lambda j, s: (0, s[3] ^ j, 0, 0))],
            scratch_shapes=[
                pltpu.VMEM((2, n * rl, cols, blk), F32),
                pltpu.VMEM((2, n, rl, cols, blk), F32),
                pltpu.VMEM((n, 2, rl, cols, blk), BF16),
                w_scratch,
                pltpu.SemaphoreType.DMA((jb,)),
            ],
        ),
        out_shape=[jax.ShapeDtypeStruct(part_shape, BF16)] * n + [jax.ShapeDtypeStruct((2, jb, 16, blk), F32)],
        name="grad",
    )(scalars, packed[0], *hid_in, tap_all, silu, slope, *cots, *w_args)
    d_parts, tap_grad = grads[:n], grads[n]
    d_recv = [turn(d_parts[k], k, f"dh{k}") for k in range(1, n)]
    d_hidden = pl.pallas_call(
        functools.partial(unpack_kernel, n, jb, blk),
        in_specs=[smem] + [vmem] * n,
        out_specs=vmem,
        out_shape=jax.ShapeDtypeStruct((tokens, chans), BF16),
        scratch_shapes=[pltpu.VMEM((n,) + part_shape, BF16)],
        name="unpack",
    )(scalars, d_parts[0], *d_recv)

    tap_grad = tap_grad.reshape(2 * jb, 16, blk)
    if fast:
        pieces = lax.all_to_all(tap_grad, "fsdp", 0, 0, tiled=True)
        mine_sum = jnp.sum(pieces, axis=0)
        theirs = turn(mine_sum, 1, "tg")
        first = jnp.where(b == 0, mine_sum, theirs)
        second = jnp.where(b == 0, theirs, mine_sum)
        share = jnp.concatenate([first, second], axis=1)
    else:
        spread = jnp.where(
            (jnp.arange(n) == b)[None, None, :, None], tap_grad.transpose(1, 0, 2)[:, :, None, :], 0.0
        ).reshape(16, chans)
        share = lax.psum(spread, "band")
        share = lax.psum_scatter(share, "fsdp", scatter_dimension=1, tiled=True)
    return (
        block_out.reshape(images, rl, cols, feats),
        d_hidden.reshape(hidden_in.shape),
        share[:9],
        share[9],
    )


def solution(mesh):
    placed = (
        P(("groups", "fsdp"), "band", None, None),
        P(None, "fsdp"),
        P("fsdp"),
        P("fsdp", None),
        P(("groups", "fsdp"), "band", None, None),
    )
    return jax.shard_map(
        body,
        mesh=mesh,
        in_specs=placed,
        out_specs=(
            P(("groups", "fsdp"), "band", None, None),
            P(("groups", "fsdp"), "band", None, None),
            P("groups", "fsdp"),
            P(("groups", "fsdp")),
        ),
        check_vma=False,
    )
```

```python
import functools

import jax
import jax.numpy as jnp
from jax import lax
from jax.experimental import pallas as pl
from jax.experimental.pallas import tpu as pltpu
from jax.sharding import PartitionSpec as P


F32 = jnp.float32
BF16 = jnp.bfloat16
LANES = 128


def up(value, step):
    return -(-value // step) * step


def pack_kernel(n, jb, blk, s_ref, x_ref, *outs):
    b = s_ref[0]
    rows, cols = outs[0].shape[2:4]
    chans = x_ref.shape[1]
    for vg in range(2):
        for jz in range(jb):
            for t in range(n):
                start = ((vg * jb + jz) * n + t) * blk
                low = start // LANES * LANES
                high = min(up(start + blk, LANES), chans)
                wide = x_ref[:, low:high].astype(F32)
                if start != low:
                    wide = pltpu.roll(wide, high - low - (start - low), 1)
                piece = wide[:, :blk].astype(BF16).reshape(rows, cols, blk)
                for k in range(n):

                    @pl.when(lax.rem(b + k, n) == t)
                    def _():
                        outs[k][vg, jz] = piece


def place_rows(n, rl, b, xs, own, received):
    for vg in range(2):
        for i in range(rl):
            xs[vg, b * rl + i] = own[vg, 0, i].astype(F32)
            for k in range(1, n):
                src = lax.rem(b - k + n, n)
                xs[vg, src * rl + i] = received[k - 1][vg, 0, i].astype(F32)


def shifted(row):
    cols = row.shape[0]
    at = lax.broadcasted_iota(jnp.int32, row.shape, 0)
    prev = jnp.where(at == 0, 0.0, pltpu.roll(row, 1, 0))
    nxt = jnp.where(at == cols - 1, 0.0, pltpu.roll(row, cols - 1, 0))
    return prev, row, nxt


def lane_tiles(blk):
    return [pl.ds(low, min(LANES, blk - low)) for low in range(0, blk, LANES)]


def conv_kernel(n, jb, rl, s_ref, own, *refs):
    received, (taps, glu, silu, slope, xs, pres) = refs[: n - 1], refs[n - 1 :]
    b, tap_mask = s_ref[0], s_ref[1]
    jz = pl.program_id(0)
    place_rows(n, rl, b, xs, own, received)
    total = n * rl
    cols, blk = own.shape[3:]
    for lanes in lane_tiles(blk):
        for vg in range(2):
            w = taps[(vg * jb + jz) ^ tap_mask, :, lanes].astype(F32)
            acc = [None] * total
            for r in range(total):
                parts = shifted(xs[vg, r, :, lanes])
                for i in range(3):
                    to = r + 1 - i
                    if 0 <= to < total:
                        term = sum(w[3 * i + j : 3 * i + j + 1] * parts[j] for j in range(3))
                        acc[to] = term + w[9:10] if acc[to] is None else acc[to] + term
                done = [r - 1] if r < total - 1 else [r - 1, r]
                for at in done:
                    if at < 0:
                        continue
                    if vg == 0:
                        pres[at] = acc[at] if acc[at].shape[1] == LANES else jnp.pad(
                            acc[at], ((0, 0), (0, LANES - acc[at].shape[1]))
                        )
                        continue
                    values, gate = pres[at][:, : acc[at].shape[1]], acc[at]
                    rel = lax.rem(at // rl - b + n, n)
                    sigma = jax.nn.sigmoid(gate)
                    act = gate * sigma
                    spot = pl.ds(at % rl * cols, cols)
                    glu[0, rel, spot, lanes] = (values * act).astype(BF16)
                    silu[0, rel, spot, lanes] = act
                    slope[0, rel, spot, lanes] = values * (sigma * (1.0 + gate * (1.0 - sigma)))


def move_weights(action, s_ref, copy, at, w_refs, w_buf, sems):
    def run(source):
        for src, slot in source(s_ref, w_refs):
            where = w_buf.at[at] if slot is None else w_buf.at[at, slot]
            getattr(pltpu.make_async_copy(src, where, sems.at[at]), action)()

    main, other = copy
    if other is None:
        run(main)
        return

    @pl.when(s_ref[2] == 1)
    def _():
        run(main)

    @pl.when(s_ref[2] == 0)
    def _():
        run(other)


def out_kernel(n, blocks, copies, n_w, first, last, s_ref, glu, *refs):
    before, refs = (None, refs) if first else (refs[0], refs[1:])
    w_refs, refs = refs[:n_w], refs[n_w:]
    outs, (w_buf, sems) = refs[:-2], refs[-2:]
    acc, outs = (outs[-1], outs[:-1]) if last else (outs[0], ())
    for at in range(len(blocks)):
        move_weights("start", s_ref, copies[at], at, w_refs, w_buf, sems)
    tokens, blk = glu.shape[2:]
    for at, k in enumerate(blocks):
        move_weights("wait", s_ref, copies[at], at, w_refs, w_buf, sems)
        part = jnp.dot(
            glu[s_ref[3] ^ k].reshape(n * tokens, blk),
            w_buf[at].reshape(blk, w_buf.shape[3]),
            preferred_element_type=F32,
        )
        if at == 0:
            acc[...] = part if before is None else before[...] + part
        else:
            acc[...] += part
    for k, out in enumerate(outs):
        out[...] = acc[k * tokens : (k + 1) * tokens, :].astype(out.dtype)


def grad_kernel(n, jb, rl, first_k, copies, n_w, aliased, s_ref, own, *refs):
    received, refs = refs[: n - 1], refs[n - 1 :]
    (taps, silu, slope), refs = refs[:3], refs[3:]
    cots, refs = refs[:n], refs[n:]
    w_refs, refs = refs[:n_w], refs[n_w + aliased :]
    outs, (tap_grad, xs, dp, dh, cot_all, w_buf, sems, cot_sems) = refs[:n], refs[n:]
    b, tap_mask = s_ref[0], s_ref[1]
    step = pl.program_id(0)
    jz = s_ref[3] ^ (step + first_k)
    tokens, blk = silu.shape[2:]
    cols = tokens // rl
    total = n * rl

    def move_cots(action):
        for k in range(n):
            where = cot_all.at[pl.ds(k * tokens, tokens)]
            getattr(pltpu.make_async_copy(cots[k], where, cot_sems.at[k]), action)()

    @pl.when(step == 0)
    def _():
        move_cots("start")
        for at in range(len(copies)):
            move_weights("start", s_ref, copies[at], at, w_refs, w_buf, sems)

    place_rows(n, rl, b, xs, own, received)

    @pl.when(step == 0)
    def _():
        move_cots("wait")

    for at in range(len(copies)):
        @pl.when(step == at)
        def _():
            move_weights("wait", s_ref, copies[at], at, w_refs, w_buf, sems)

    d_glu = lax.dot_general(
        cot_all[...],
        w_buf[step].reshape(blk, w_buf.shape[3]),
        (((1,), (1,)), ((), ())),
        preferred_element_type=F32,
    ).reshape(n, tokens, blk)
    dp[0] = (d_glu * silu[0]).astype(BF16).astype(F32).reshape(n, rl, cols, blk)
    dp[1] = (d_glu * slope[0]).astype(BF16).astype(F32).reshape(n, rl, cols, blk)

    def fold(value):
        return jnp.sum(value.reshape(cols // 8, 8, value.shape[1]), axis=0)

    for vg in range(2):
        for lanes in lane_tiles(blk):
            w = taps[(vg * jb + jz) ^ tap_mask, :, lanes].astype(F32)
            acc = [None] * total
            sums = [None] * 10
            for r in range(total):
                row = dp[vg, lax.rem(r // rl - b + n, n), r % rl, :, lanes]
                seen = shifted(row)
                part = fold(row)
                sums[9] = part if sums[9] is None else sums[9] + part
                for i in range(3):
                    to = r - 1 + i
                    if not 0 <= to < total:
                        continue
                    x = xs[vg, to, :, lanes]
                    term = sum(w[3 * i + j : 3 * i + j + 1] * seen[2 - j] for j in range(3))
                    acc[to] = term if acc[to] is None else acc[to] + term
                    for j in range(3):
                        part = fold(x * seen[2 - j])
                        tap = 3 * i + j
                        sums[tap] = part if sums[tap] is None else sums[tap] + part
                for to in [r - 1] if r < total - 1 else [r - 1, r]:
                    if to >= 0:
                        rel = lax.rem(to // rl - b + n, n)
                        dh[rel, vg, to % rl, :, lanes] = acc[to].astype(BF16)
            tap_grad[vg, 0, :10, lanes] = jnp.concatenate(
                [jnp.sum(v, axis=0, keepdims=True) for v in sums], axis=0
            )
    for k in range(n):
        for vg in range(2):
            outs[k][vg, 0] = dh[k, vg]


def unpack_kernel(n, jb, blk, sizes, s_ref, *refs):
    ins, out, held = refs[:-2], refs[-2], refs[-1]
    b = s_ref[0]
    rl, cols = ins[0].shape[2:4]
    done = 0
    for c, size in enumerate(sizes):
        for k in range(n):
            for at in range(size):
                held[lax.rem(b - k + n, n), :, s_ref[3] ^ (done + at)] = ins[c * n + k][:, at]
        done += size
    for vg in range(2):
        for jz in range(jb):
            for t in range(n):
                start = ((vg * jb + jz) * n + t) * blk
                out[:, start : start + blk] = held[t, vg, jz].reshape(rl * cols, blk)


def unit(hidden_in, tap_weights, tap_bias, w_out, cotangent):
    groups, shards, n = (lax.axis_size(a) for a in ("groups", "fsdp", "band"))
    images, rl, cols, chans = hidden_in.shape
    blk = w_out.shape[0]
    jb = shards // n
    feats = w_out.shape[1]
    tokens = rl * cols
    g, f, b = (lax.axis_index(a) for a in ("groups", "fsdp", "band"))
    fast = n == 2 and groups == 2 and shards % 4 == 0 and shards & (shards - 1) == 0 and blk % 32 == 0
    assert images == 1 and shards % n == 0

    tap_block = jnp.concatenate(
        [tap_weights, tap_bias[None], jnp.zeros((6, tap_bias.shape[0]), BF16)], axis=0
    )
    if fast:
        scalars = jnp.stack([b, f, jnp.where(f % 2 == b, 1, 0), f // n, g]).astype(jnp.int32)
    else:
        scalars = jnp.stack([b, 0 * f, 0 * f + 1, 0 * f, g]).astype(jnp.int32)

    if fast:
        every = ("groups", "fsdp", "band")
        zr = jb

        def across(x, flip):
            pairs = [
                (s * n + t, (s ^ flip) * n + t)
                for s in range(shards) for t in range(n) if flip == 1 or s % 2 == t
            ]
            return lax.ppermute(x, ("fsdp", "band"), pairs)

        def other_group(x):
            size = shards * n
            pairs = [
                (p * size + s * n + t, (1 - p) * size + s * n + t)
                for p in range(2) for s in range(shards) for t in range(n) if s % 2 == t
            ]
            return lax.ppermute(x, every, pairs)

        half = lax.dynamic_slice_in_dim(w_out, g * (blk // 2), blk // 2, 0)
        mine = {0: half}
        order = []
        bit = zr // 2
        while bit:
            order.append(bit)
            bit //= 2
        for bit in order:
            for k in list(mine):
                mine[k ^ bit] = across(mine[k], 2 * bit)
        w_parts = []
        for k in range(zr):
            if k == 0:
                w_parts.append(([w.reshape(2, blk // 2, feats) for w in (w_out, across(w_out, 1))], False))
            else:
                a, y = mine[k], other_group(mine[k])
                w_parts.append(([a, y, across(a, 1), across(y, 1)], True))
        parts = 2
    else:
        w_all = lax.all_gather(w_out, "fsdp", axis=0, tiled=True).reshape(jb, n, 1, blk, feats)
        w_args = [lax.dynamic_index_in_dim(w_all, b, 1, keepdims=False)]
        copies = [(lambda s, w, k=k: [(w[0].at[k], None)], None) for k in range(jb)]
        parts = 1

    if fast:
        tap_all = lax.dynamic_slice_in_dim(tap_block, b * blk, blk, 1)[None]
        step = 1
        while step < shards:
            other = lax.ppermute(tap_all, "fsdp", [(i, i ^ step) for i in range(shards)])
            tap_all = jnp.concatenate([tap_all, other], axis=0)
            step *= 2
    else:
        tap_all = lax.all_gather(tap_block, "fsdp", axis=1, tiled=True)
        tap_all = tap_all.reshape(16, 2 * jb, n, blk)
        tap_all = lax.dynamic_index_in_dim(tap_all, b, 2, keepdims=False).transpose(1, 0, 2)

    vmem = pl.BlockSpec(memory_space=pltpu.VMEM)
    smem = pl.BlockSpec(memory_space=pltpu.SMEM)
    part_shape = (2, jb, rl, cols, blk)
    packed = pl.pallas_call(
        functools.partial(pack_kernel, n, jb, blk),
        out_shape=[jax.ShapeDtypeStruct(part_shape, BF16)] * n,
        in_specs=[smem, vmem],
        out_specs=[vmem] * n,
        name="pack",
    )(scalars, hidden_in.reshape(tokens, chans))

    def turn(x, k):
        return lax.ppermute(x, "band", [(i, (i + k) % n) for i in range(n)])

    hid_in = [turn(packed[k], k) for k in range(1, n)]
    cots = [cotangent] + [turn(cotangent, n - k) for k in range(1, n)]
    cots = [c.reshape(tokens, feats) for c in cots]

    part_spec = pl.BlockSpec((2, 1, rl, cols, blk), lambda j, s: (0, j, 0, 0, 0))
    tap_spec = pl.BlockSpec((2 * jb, 16, blk), lambda j, s: (0, 0, 0))
    act_spec = pl.BlockSpec((1, n, tokens, blk), lambda j, s: (j, 0, 0, 0))
    act_shape = (jb, n, tokens, blk)
    glu, silu, slope = pl.pallas_call(
        functools.partial(conv_kernel, n, jb, rl),
        grid_spec=pltpu.PrefetchScalarGridSpec(
            num_scalar_prefetch=1,
            grid=(jb,),
            in_specs=[part_spec] * n + [tap_spec],
            out_specs=[act_spec] * 3,
            scratch_shapes=[
                pltpu.VMEM((2, n * rl, cols, blk), F32),
                pltpu.VMEM((n * rl, cols, LANES), F32),
            ],
        ),
        out_shape=[
            jax.ShapeDtypeStruct(act_shape, BF16),
            jax.ShapeDtypeStruct(act_shape, F32),
            jax.ShapeDtypeStruct(act_shape, F32),
        ],
        name="conv",
    )(scalars, packed[0], *hid_in, tap_all)

    any_spec = pl.BlockSpec(memory_space=pl.ANY)
    chunks, done = [], 0
    for size in CHUNKS if fast and sum(CHUNKS) == jb else (jb,):
        chunks.append(range(done, done + size))
        done += size

    def weights_of(blocks):
        if not fast:
            return w_args, copies
        args, moves = [], []
        for k in blocks:
            arrays, halves = w_parts[k]
            base = len(args)
            args += arrays
            if halves:
                moves.append((
                    lambda s, w, i=base: [(w[i], s[4]), (w[i + 1], 1 - s[4])],
                    lambda s, w, i=base + 2: [(w[i], s[4]), (w[i + 1], 1 - s[4])],
                ))
            else:
                moves.append((
                    lambda s, w, i=base: [(w[i], None)],
                    lambda s, w, i=base + 1: [(w[i], None)],
                ))
        return args, moves

    partial = None
    for c, blocks in enumerate(chunks):
        args, moves = weights_of(blocks)
        first, last = c == 0, c == len(chunks) - 1
        shapes = [jax.ShapeDtypeStruct((tokens, feats), F32 if k == 0 else BF16) for k in range(n)]
        total_shape = jax.ShapeDtypeStruct((n * tokens, feats), F32)
        scratch = [
            pltpu.VMEM((len(blocks), parts, blk // parts, feats), BF16),
            pltpu.SemaphoreType.DMA((len(blocks),)),
        ]
        if last:
            scratch = [pltpu.VMEM((n * tokens, feats), F32)] + scratch
        partial = pl.pallas_call(
            functools.partial(out_kernel, n, blocks, moves, len(args), first, last),
            in_specs=[smem] + [vmem] * (1 if first else 2) + [any_spec] * len(args),
            out_specs=[vmem] * n if last else vmem,
            out_shape=shapes if last else total_shape,
            scratch_shapes=scratch,
        )(scalars, glu, *([] if first else [partial]), *args)
    partial = [p.reshape(cotangent.shape) for p in partial]
    block_out = partial[0]
    for k in range(1, n):
        block_out = block_out + turn(partial[k], k).astype(F32)
    block_out = block_out.astype(BF16)

    tap_grad, d_parts = None, []
    for blocks in chunks:
        args, moves = weights_of(blocks)
        at = lambda j, s, lo=blocks[0]: s[3] ^ (j + lo)
        part_at = pl.BlockSpec((2, 1, rl, cols, blk), lambda j, s, at=at: (0, at(j, s), 0, 0, 0))
        act_at = pl.BlockSpec((1, n, tokens, blk), lambda j, s, at=at: (at(j, s), 0, 0, 0))
        aliased = 0 if tap_grad is None else 1
        outs = pl.pallas_call(
            functools.partial(grad_kernel, n, jb, rl, blocks[0], moves, len(args), aliased),
            grid_spec=pltpu.PrefetchScalarGridSpec(
                num_scalar_prefetch=1,
                grid=(len(blocks),),
                in_specs=[part_at] * n + [tap_spec, act_at, act_at] + [any_spec] * (n + len(args) + aliased),
                out_specs=[part_spec] * n
                + [pl.BlockSpec((2, 1, 16, blk), lambda j, s, at=at: (0, at(j, s), 0, 0))],
                scratch_shapes=[
                    pltpu.VMEM((2, n * rl, cols, blk), F32),
                    pltpu.VMEM((2, n, rl, cols, blk), F32),
                    pltpu.VMEM((n, 2, rl, cols, blk), BF16),
                    pltpu.VMEM((n * tokens, feats), BF16),
                    pltpu.VMEM((len(blocks), parts, blk // parts, feats), BF16),
                    pltpu.SemaphoreType.DMA((len(blocks),)),
                    pltpu.SemaphoreType.DMA((n,)),
                ],
            ),
            out_shape=[jax.ShapeDtypeStruct((2, len(blocks), rl, cols, blk), BF16)] * n
            + [jax.ShapeDtypeStruct((2, jb, 16, blk), F32)],
            input_output_aliases={4 + 2 * n + len(args): n} if aliased else {},
        )(
            scalars, packed[0], *hid_in, tap_all, silu, slope, *cots, *args,
            *([tap_grad] if aliased else []),
        )
        tap_grad = outs[n]
        d_parts += [outs[0]] + [turn(outs[k], k) for k in range(1, n)]
    d_hidden = pl.pallas_call(
        functools.partial(unpack_kernel, n, jb, blk, [len(c) for c in chunks]),
        in_specs=[smem] + [vmem] * len(d_parts),
        out_specs=vmem,
        out_shape=jax.ShapeDtypeStruct((tokens, chans), BF16),
        scratch_shapes=[pltpu.VMEM((n,) + part_shape, BF16)],
        name="unpack",
    )(scalars, *d_parts)

    tap_grad = tap_grad.reshape(2 * jb, 16, blk)
    if fast:
        pieces = lax.all_to_all(tap_grad, "fsdp", 0, 0, tiled=True)
        mine_sum = jnp.sum(pieces, axis=0)
        theirs = turn(mine_sum, 1)
        first = jnp.where(b == 0, mine_sum, theirs)
        second = jnp.where(b == 0, theirs, mine_sum)
        share = jnp.concatenate([first, second], axis=1)
    else:
        spread = jnp.where(
            (jnp.arange(n) == b)[None, None, :, None], tap_grad.transpose(1, 0, 2)[:, :, None, :], 0.0
        ).reshape(16, chans)
        share = lax.psum(spread, "band")
        share = lax.psum_scatter(share, "fsdp", scatter_dimension=1, tiled=True)
    return (
        block_out,
        d_hidden.reshape(hidden_in.shape),
        share[:9],
        share[9],
    )


CHUNKS = (3, 1)


def solution(mesh):
    placed = (
        P(("groups", "fsdp"), "band", None, None),
        P(None, "fsdp"),
        P("fsdp"),
        P("fsdp", None),
        P(("groups", "fsdp"), "band", None, None),
    )
    return jax.shard_map(
        unit,
        mesh=mesh,
        in_specs=placed,
        out_specs=(
            P(("groups", "fsdp"), "band", None, None),
            P(("groups", "fsdp"), "band", None, None),
            P("groups", "fsdp"),
            P(("groups", "fsdp")),
        ),
        check_vma=False,
    )
```

```python
import functools

import jax
import jax.numpy as jnp
from jax import lax
from jax.experimental import pallas as pl
from jax.experimental.pallas import tpu as pltpu
from jax.sharding import PartitionSpec as P


F32 = jnp.float32
BF16 = jnp.bfloat16
LANES = 128


def up(value, step):
    return -(-value // step) * step


def pack_kernel(n, jb, blk, s_ref, x_ref, *outs):
    b = s_ref[0]
    chans = x_ref.shape[1]
    for vg in range(2):
        for jz in range(jb):
            for t in range(n):
                start = ((vg * jb + jz) * n + t) * blk
                low = start // LANES * LANES
                high = min(up(start + blk, LANES), chans)
                wide = x_ref[:, low:high].astype(F32)
                if start != low:
                    wide = pltpu.roll(wide, high - low - (start - low), 1)
                piece = wide[:, :blk].astype(BF16)
                for k in range(n):

                    @pl.when(lax.rem(b + k, n) == t)
                    def _():
                        outs[k][vg, jz, 0] = piece


def place_rows(n, rl, b, xs, own, received):
    for vg in range(2):
        for i in range(rl):
            xs[vg, b * rl + i] = own[vg, 0, i].astype(F32)
            for k in range(1, n):
                src = lax.rem(b - k + n, n)
                xs[vg, src * rl + i] = received[k - 1][vg, 0, i].astype(F32)


def shifted(row):
    cols = row.shape[0]
    at = lax.broadcasted_iota(jnp.int32, row.shape, 0)
    prev = jnp.where(at == 0, 0.0, pltpu.roll(row, 1, 0))
    nxt = jnp.where(at == cols - 1, 0.0, pltpu.roll(row, cols - 1, 0))
    return prev, row, nxt


def lane_tiles(blk):
    return [pl.ds(low, min(LANES, blk - low)) for low in range(0, blk, LANES)]


def conv_kernel(n, jb, rl, s_ref, own, *refs):
    received, (taps, glu, silu, slope, xs, pres) = refs[: n - 1], refs[n - 1 :]
    b, tap_mask = s_ref[0], s_ref[1]
    jz = pl.program_id(0)
    place_rows(n, rl, b, xs, own, received)
    total = n * rl
    cols, blk = own.shape[3:]
    for lanes in lane_tiles(blk):
        for vg in range(2):
            w = taps[(vg * jb + jz) ^ tap_mask, :, lanes].astype(F32)
            acc = [None] * total
            for r in range(total):
                parts = shifted(xs[vg, r, :, lanes])
                for i in range(3):
                    to = r + 1 - i
                    if 0 <= to < total:
                        term = sum(w[3 * i + j : 3 * i + j + 1] * parts[j] for j in range(3))
                        acc[to] = term + w[9:10] if acc[to] is None else acc[to] + term
                done = [r - 1] if r < total - 1 else [r - 1, r]
                for at in done:
                    if at < 0:
                        continue
                    if vg == 0:
                        pres[at] = acc[at] if acc[at].shape[1] == LANES else jnp.pad(
                            acc[at], ((0, 0), (0, LANES - acc[at].shape[1]))
                        )
                        continue
                    values, gate = pres[at][:, : acc[at].shape[1]], acc[at]
                    rel = lax.rem(at // rl - b + n, n)
                    sigma = jax.nn.sigmoid(gate)
                    act = gate * sigma
                    spot = pl.ds(at % rl * cols, cols)
                    glu[0, rel, spot, lanes] = (values * act).astype(BF16)
                    silu[0, rel, spot, lanes] = act
                    slope[0, rel, spot, lanes] = values * (sigma * (1.0 + gate * (1.0 - sigma)))


def move_weights(action, s_ref, copy, at, w_refs, w_buf, sems):
    def run(source):
        for src, slot in source(s_ref, w_refs):
            where = w_buf.at[at] if slot is None else w_buf.at[at, slot]
            getattr(pltpu.make_async_copy(src, where, sems.at[at]), action)()

    main, other = copy
    if other is None:
        run(main)
        return

    @pl.when(s_ref[2] == 1)
    def _():
        run(main)

    @pl.when(s_ref[2] == 0)
    def _():
        run(other)


def out_kernel(n, copies, n_w, s_ref, glu, *refs):
    w_refs, outs, (acc, w_buf, sems) = refs[:n_w], refs[n_w:-3], refs[-3:]
    for k, copy in enumerate(copies):
        move_weights("start", s_ref, copy, k, w_refs, w_buf, sems)
    tokens, blk = glu.shape[2:]
    for k, copy in enumerate(copies):
        move_weights("wait", s_ref, copy, k, w_refs, w_buf, sems)
        part = jnp.dot(
            glu[s_ref[3] ^ k].reshape(n * tokens, blk),
            w_buf[k].reshape(blk, w_buf.shape[3]),
            preferred_element_type=F32,
        )
        if k == 0:
            acc[...] = part
        else:
            acc[...] += part
    for k, out in enumerate(outs):
        out[...] = acc[k * tokens : (k + 1) * tokens, :].astype(out.dtype)


def grad_kernel(n, jb, rl, blocks, copies, n_w, aliased, s_ref, own, *refs):
    received, refs = refs[: n - 1], refs[n - 1 :]
    (taps, silu, slope), refs = refs[:3], refs[3:]
    cots, refs = refs[:n], refs[n:]
    w_refs, refs = refs[:n_w], refs[n_w + aliased :]
    outs, (tap_grad, xs, dp, dh, cot_all, w_buf, sems, cot_sems) = refs[:n], refs[n:]
    b, tap_mask = s_ref[0], s_ref[1]
    step = pl.program_id(0)
    jz = s_ref[3] ^ (step * blocks.step + blocks.start)
    tokens, blk = silu.shape[2:]
    cols = tokens // rl
    total = n * rl

    def move_cots(action):
        for k in range(n):
            where = cot_all.at[pl.ds(k * tokens, tokens)]
            getattr(pltpu.make_async_copy(cots[k], where, cot_sems.at[k]), action)()

    @pl.when(step == 0)
    def _():
        move_cots("start")
        for at in range(len(copies)):
            move_weights("start", s_ref, copies[at], at, w_refs, w_buf, sems)

    place_rows(n, rl, b, xs, own, received)

    @pl.when(step == 0)
    def _():
        move_cots("wait")

    for at in range(len(copies)):
        @pl.when(step == at)
        def _():
            move_weights("wait", s_ref, copies[at], at, w_refs, w_buf, sems)

    d_glu = lax.dot_general(
        cot_all[...],
        w_buf[step].reshape(blk, w_buf.shape[3]),
        (((1,), (1,)), ((), ())),
        preferred_element_type=F32,
    ).reshape(n, tokens, blk)
    dp[0] = (d_glu * silu[0]).astype(BF16).astype(F32).reshape(n, rl, cols, blk)
    dp[1] = (d_glu * slope[0]).astype(BF16).astype(F32).reshape(n, rl, cols, blk)

    def fold(value):
        return jnp.sum(value.reshape(cols // 8, 8, value.shape[1]), axis=0)

    for vg in range(2):
        for lanes in lane_tiles(blk):
            w = taps[(vg * jb + jz) ^ tap_mask, :, lanes].astype(F32)
            acc = [None] * total
            sums = [None] * 10
            for r in range(total):
                row = dp[vg, lax.rem(r // rl - b + n, n), r % rl, :, lanes]
                seen = shifted(row)
                part = fold(row)
                sums[9] = part if sums[9] is None else sums[9] + part
                for i in range(3):
                    to = r - 1 + i
                    if not 0 <= to < total:
                        continue
                    x = xs[vg, to, :, lanes]
                    term = sum(w[3 * i + j : 3 * i + j + 1] * seen[2 - j] for j in range(3))
                    acc[to] = term if acc[to] is None else acc[to] + term
                    for j in range(3):
                        part = fold(x * seen[2 - j])
                        tap = 3 * i + j
                        sums[tap] = part if sums[tap] is None else sums[tap] + part
                for to in [r - 1] if r < total - 1 else [r - 1, r]:
                    if to >= 0:
                        rel = lax.rem(to // rl - b + n, n)
                        dh[rel, vg, to % rl, :, lanes] = acc[to].astype(BF16)
            tap_grad[vg, 0, :10, lanes] = jnp.concatenate(
                [jnp.sum(v, axis=0, keepdims=True) for v in sums], axis=0
            )
    for k in range(n):
        for vg in range(2):
            outs[k][vg, 0] = dh[k, vg]


def unpack_kernel(n, jb, blk, chunks, s_ref, *refs):
    ins, out, held = refs[:-2], refs[-2], refs[-1]
    b = s_ref[0]
    for c, blocks in enumerate(chunks):
        for k in range(n):
            for at, kz in enumerate(blocks):
                held[lax.rem(b - k + n, n), :, s_ref[3] ^ kz] = ins[c * n + k][:, at, 0]
    for vg in range(2):
        for jz in range(jb):
            for t in range(n):
                start = ((vg * jb + jz) * n + t) * blk
                out[:, start : start + blk] = held[t, vg, jz]


def unit(hidden_in, tap_weights, tap_bias, w_out, cotangent):
    groups, shards, n = (lax.axis_size(a) for a in ("groups", "fsdp", "band"))
    images, rl, cols, chans = hidden_in.shape
    blk = w_out.shape[0]
    jb = shards // n
    feats = w_out.shape[1]
    tokens = rl * cols
    g, f, b = (lax.axis_index(a) for a in ("groups", "fsdp", "band"))
    fast = n == 2 and groups == 2 and shards % 4 == 0 and shards & (shards - 1) == 0 and blk % 32 == 0
    assert images == 1 and shards % n == 0

    tap_block = jnp.concatenate(
        [tap_weights, tap_bias[None], jnp.zeros((6, tap_bias.shape[0]), BF16)], axis=0
    )
    if fast:
        scalars = jnp.stack([b, f // 2 * 2 + 1 - b, jnp.where(f % 2 == b, 1, 0), f // n, g]).astype(jnp.int32)
    else:
        scalars = jnp.stack([b, 0 * f, 0 * f + 1, 0 * f, 0 * g]).astype(jnp.int32)

    vmem = pl.BlockSpec(memory_space=pltpu.VMEM)
    smem = pl.BlockSpec(memory_space=pltpu.SMEM)
    any_spec = pl.BlockSpec(memory_space=pl.ANY)
    part_shape = (2, jb, rl, cols, blk)
    packed = pl.pallas_call(
        functools.partial(pack_kernel, n, jb, blk),
        grid_spec=pltpu.PrefetchScalarGridSpec(
            num_scalar_prefetch=1,
            grid=(rl,),
            in_specs=[pl.BlockSpec((cols, chans), lambda i, s: (i, 0))],
            out_specs=[pl.BlockSpec((2, jb, 1, cols, blk), lambda i, s: (0, 0, i, 0, 0))] * n,
        ),
        out_shape=[jax.ShapeDtypeStruct(part_shape, BF16)] * n,
        name="pack",
    )(scalars, hidden_in.reshape(tokens, chans))

    if fast:
        every = ("groups", "fsdp", "band")
        zr = jb

        def across(x, flip):
            pairs = [
                (s * n + t, (s ^ flip) * n + t)
                for s in range(shards) for t in range(n) if flip == 1 or s % 2 == t
            ]
            return lax.ppermute(x, ("fsdp", "band"), pairs)

        def other_group(x):
            size = shards * n
            pairs = [
                (p * size + s * n + t, (1 - p) * size + s * n + t)
                for p in range(2) for s in range(shards) for t in range(n) if s % 2 == t
            ]
            return lax.ppermute(x, every, pairs)

        mine = {0: lax.dynamic_slice_in_dim(w_out, g * (blk // 2), blk // 2, 0)}
        order = []
        bit = zr // 2
        while bit:
            order.append(bit)
            bit //= 2
        for bit in order:
            for k in list(mine):
                mine[k ^ bit] = across(mine[k], 2 * bit)
        w_parts = []
        for k in range(zr):
            if k == 0:
                pair = [w_out, across(w_out, 1)]
                w_parts.append(([w.reshape(2, blk // 2, feats) for w in pair], False))
            else:
                a, y = mine[k], other_group(mine[k])
                w_parts.append(([a, y, across(a, 1), across(y, 1)], True))
        parts = 2
    else:
        w_all = lax.all_gather(w_out, "fsdp", axis=0, tiled=True).reshape(jb, n, 1, blk, feats)
        w_args = [lax.dynamic_index_in_dim(w_all, b, 1, keepdims=False)]
        copies = [(lambda s, w, k=k: [(w[0].at[k], None)], None) for k in range(jb)]
        parts = 1

    if fast:
        tap_own = lax.dynamic_slice_in_dim(tap_block, b * blk, blk, 1)
        tap_pair = jnp.stack([tap_own, across(tap_own, 1)])
        tap_all = [tap_pair]
        for k in range(1, zr):
            pairs = [
                (s * n + t, (s ^ 2 * k) * n + t) for s in range(shards) for t in range(n) if s % 2 != t
            ]
            tap_all.append(lax.ppermute(tap_pair, ("fsdp", "band"), pairs))
        tap_all = jnp.concatenate(tap_all, axis=0)
        tap_all = jnp.where(f % 2 == b, across(tap_all, 1), tap_all)
    else:
        tap_all = lax.all_gather(tap_block, "fsdp", axis=1, tiled=True)
        tap_all = tap_all.reshape(16, 2 * jb, n, blk)
        tap_all = lax.dynamic_index_in_dim(tap_all, b, 2, keepdims=False).transpose(1, 0, 2)

    def turn(x, k):
        return lax.ppermute(x, "band", [(i, (i + k) % n) for i in range(n)])

    hid_in = [turn(packed[k], k) for k in range(1, n)]
    cots = [cotangent] + [turn(cotangent, n - k) for k in range(1, n)]
    cots = [c.reshape(tokens, feats) for c in cots]

    part_spec = pl.BlockSpec((2, 1, rl, cols, blk), lambda j, s: (0, j, 0, 0, 0))
    tap_spec = pl.BlockSpec((2 * jb, 16, blk), lambda j, s: (0, 0, 0))
    act_spec = pl.BlockSpec((1, n, tokens, blk), lambda j, s: (j, 0, 0, 0))
    act_shape = (jb, n, tokens, blk)
    glu, silu, slope = pl.pallas_call(
        functools.partial(conv_kernel, n, jb, rl),
        grid_spec=pltpu.PrefetchScalarGridSpec(
            num_scalar_prefetch=1,
            grid=(jb,),
            in_specs=[part_spec] * n + [tap_spec],
            out_specs=[act_spec] * 3,
            scratch_shapes=[
                pltpu.VMEM((2, n * rl, cols, blk), F32),
                pltpu.VMEM((n * rl, cols, LANES), F32),
            ],
        ),
        out_shape=[
            jax.ShapeDtypeStruct(act_shape, BF16),
            jax.ShapeDtypeStruct(act_shape, F32),
            jax.ShapeDtypeStruct(act_shape, F32),
        ],
        name="conv",
    )(scalars, packed[0], *hid_in, tap_all)

    chunks = [range(jb - 1), range(jb - 1, jb)] if fast else [range(jb)]

    def weights_of(blocks):
        if not fast:
            return w_args, copies
        args, moves = [], []
        for k in blocks:
            arrays, halves = w_parts[k]
            base = len(args)
            args += arrays
            if halves:
                moves.append((
                    lambda s, w, i=base: [(w[i], s[4]), (w[i + 1], 1 - s[4])],
                    lambda s, w, i=base + 2: [(w[i], s[4]), (w[i + 1], 1 - s[4])],
                ))
            else:
                moves.append((
                    lambda s, w, i=base: [(w[i], None)],
                    lambda s, w, i=base + 1: [(w[i], None)],
                ))
        return args, moves

    args, moves = weights_of(range(jb))
    partial = pl.pallas_call(
        functools.partial(out_kernel, n, moves, len(args)),
        in_specs=[smem, vmem] + [any_spec] * len(args),
        out_specs=[vmem] * n,
        out_shape=[jax.ShapeDtypeStruct((tokens, feats), F32 if k == 0 else BF16) for k in range(n)],
        scratch_shapes=[
            pltpu.VMEM((n * tokens, feats), F32),
            pltpu.VMEM((jb, parts, blk // parts, feats), BF16),
            pltpu.SemaphoreType.DMA((jb,)),
        ],
        name="project",
    )(scalars, glu, *args)
    partial = [p.reshape(cotangent.shape) for p in partial]
    block_out = partial[0]
    others = [turn(partial[k], k) for k in range(1, n)]
    for other in others:
        block_out = block_out + other.astype(F32)
    block_out = block_out.astype(BF16)

    tap_grad, d_parts = None, []
    for blocks in chunks:
        args, moves = weights_of(blocks)
        at = lambda j, s, c=blocks: s[3] ^ (j * c.step + c.start)
        part_at = pl.BlockSpec((2, 1, rl, cols, blk), lambda j, s, at=at: (0, at(j, s), 0, 0, 0))
        act_at = pl.BlockSpec((1, n, tokens, blk), lambda j, s, at=at: (at(j, s), 0, 0, 0))
        aliased = 0 if tap_grad is None else 1
        outs = pl.pallas_call(
            functools.partial(grad_kernel, n, jb, rl, blocks, moves, len(args), aliased),
            grid_spec=pltpu.PrefetchScalarGridSpec(
                num_scalar_prefetch=1,
                grid=(len(blocks),),
                in_specs=[part_at] * n + [tap_spec, act_at, act_at] + [any_spec] * (n + len(args) + aliased),
                out_specs=[part_spec] * n
                + [pl.BlockSpec((2, 1, 16, blk), lambda j, s, at=at: (0, at(j, s), 0, 0))],
                scratch_shapes=[
                    pltpu.VMEM((2, n * rl, cols, blk), F32),
                    pltpu.VMEM((2, n, rl, cols, blk), F32),
                    pltpu.VMEM((n, 2, rl, cols, blk), BF16),
                    pltpu.VMEM((n * tokens, feats), BF16),
                    pltpu.VMEM((len(blocks), parts, blk // parts, feats), BF16),
                    pltpu.SemaphoreType.DMA((len(blocks),)),
                    pltpu.SemaphoreType.DMA((n,)),
                ],
            ),
            out_shape=[jax.ShapeDtypeStruct((2, len(blocks), rl, cols, blk), BF16)] * n
            + [jax.ShapeDtypeStruct((2, jb, 16, blk), F32)],
            input_output_aliases={4 + 2 * n + len(args): n} if aliased else {},
        )(
            scalars, packed[0], *hid_in, tap_all, silu, slope, *cots, *args,
            *([tap_grad] if aliased else []),
        )
        tap_grad = outs[n]
        d_parts += [outs[0]] + [turn(outs[k], k) for k in range(1, n)]
    d_hidden = pl.pallas_call(
        functools.partial(unpack_kernel, n, jb, blk, chunks),
        grid_spec=pltpu.PrefetchScalarGridSpec(
            num_scalar_prefetch=1,
            grid=(rl,),
            in_specs=[
                pl.BlockSpec((2, p.shape[1], 1, cols, blk), lambda i, s: (0, 0, i, 0, 0)) for p in d_parts
            ],
            out_specs=pl.BlockSpec((cols, chans), lambda i, s: (i, 0)),
            scratch_shapes=[pltpu.VMEM((n, 2, jb, cols, blk), BF16)],
        ),
        out_shape=jax.ShapeDtypeStruct((tokens, chans), BF16),
        name="unpack",
    )(scalars, *d_parts)

    tap_grad = tap_grad.reshape(2 * jb, 16, blk)
    if fast:
        pieces = lax.all_to_all(tap_grad, "fsdp", 0, 0, tiled=True)
        mine_sum = jnp.sum(pieces, axis=0)
        theirs = turn(mine_sum, 1)
        first = jnp.where(b == 0, mine_sum, theirs)
        second = jnp.where(b == 0, theirs, mine_sum)
        share = jnp.concatenate([first, second], axis=1)
    else:
        spread = jnp.where(
            (jnp.arange(n) == b)[None, None, :, None], tap_grad.transpose(1, 0, 2)[:, :, None, :], 0.0
        ).reshape(16, chans)
        share = lax.psum(spread, "band")
        share = lax.psum_scatter(share, "fsdp", scatter_dimension=1, tiled=True)
    return (
        block_out,
        d_hidden.reshape(hidden_in.shape),
        share[:9],
        share[9],
    )


def solution(mesh):
    placed = (
        P(("groups", "fsdp"), "band", None, None),
        P(None, "fsdp"),
        P("fsdp"),
        P("fsdp", None),
        P(("groups", "fsdp"), "band", None, None),
    )
    return jax.shard_map(
        unit,
        mesh=mesh,
        in_specs=placed,
        out_specs=(
            P(("groups", "fsdp"), "band", None, None),
            P(("groups", "fsdp"), "band", None, None),
            P("groups", "fsdp"),
            P(("groups", "fsdp")),
        ),
        check_vma=False,
    )
```

```python
import functools

import jax
import jax.numpy as jnp
from jax import lax
from jax.experimental import pallas as pl
from jax.experimental.pallas import tpu as pltpu
from jax.sharding import PartitionSpec as P


F32 = jnp.float32
BF16 = jnp.bfloat16
LANES = 128


def up(value, step):
    return -(-value // step) * step


def pack_kernel(n, jb, blk, s_ref, x_ref, *refs):
    outs, held = refs[:-1], refs[-1]
    b = s_ref[0]
    chans = x_ref.shape[1]
    for vg in range(2):
        for jz in range(jb):
            for t in range(n):
                start = ((vg * jb + jz) * n + t) * blk
                low = start // LANES * LANES
                high = min(up(start + blk, LANES), chans)
                wide = x_ref[:, low:high].astype(F32)
                if start != low:
                    wide = pltpu.roll(wide, high - low - (start - low), 1)
                held[lax.rem(t - b + n, n), vg, jz] = wide[:, :blk].astype(BF16)
    for k in range(n):
        outs[k][:, :, 0] = held[k]


def place_rows(n, rl, b, xs, own, received):
    for vg in range(2):
        for i in range(rl):
            xs[vg, b * rl + i] = own[vg, 0, i].astype(F32)
            for k in range(1, n):
                src = lax.rem(b - k + n, n)
                xs[vg, src * rl + i] = received[k - 1][vg, 0, i].astype(F32)


def shifted(row):
    cols = row.shape[0]
    at = lax.broadcasted_iota(jnp.int32, row.shape, 0)
    prev = jnp.where(at == 0, 0.0, pltpu.roll(row, 1, 0))
    nxt = jnp.where(at == cols - 1, 0.0, pltpu.roll(row, cols - 1, 0))
    return prev, row, nxt


def lane_tiles(blk):
    return [pl.ds(low, min(LANES, blk - low)) for low in range(0, blk, LANES)]


def conv_kernel(n, jb, rl, s_ref, own, *refs):
    received, (taps, glu, silu, slope, xs, pres) = refs[: n - 1], refs[n - 1 :]
    b, tap_mask = s_ref[0], s_ref[1]
    jz = pl.program_id(0)
    place_rows(n, rl, b, xs, own, received)
    total = n * rl
    cols, blk = own.shape[3:]
    for lanes in lane_tiles(blk):
        for vg in range(2):
            w = taps[(vg * jb + jz) ^ tap_mask, :, lanes].astype(F32)
            acc = [None] * total
            for r in range(total):
                parts = shifted(xs[vg, r, :, lanes])
                for i in range(3):
                    to = r + 1 - i
                    if 0 <= to < total:
                        term = sum(w[3 * i + j : 3 * i + j + 1] * parts[j] for j in range(3))
                        acc[to] = term + w[9:10] if acc[to] is None else acc[to] + term
                done = [r - 1] if r < total - 1 else [r - 1, r]
                for at in done:
                    if at < 0:
                        continue
                    if vg == 0:
                        pres[at] = acc[at] if acc[at].shape[1] == LANES else jnp.pad(
                            acc[at], ((0, 0), (0, LANES - acc[at].shape[1]))
                        )
                        continue
                    values, gate = pres[at][:, : acc[at].shape[1]], acc[at]
                    rel = lax.rem(at // rl - b + n, n)
                    sigma = jax.nn.sigmoid(gate)
                    act = gate * sigma
                    spot = pl.ds(at % rl * cols, cols)
                    glu[0, rel, spot, lanes] = (values * act).astype(BF16)
                    silu[0, rel, spot, lanes] = act
                    slope[0, rel, spot, lanes] = values * (sigma * (1.0 + gate * (1.0 - sigma)))


def move_weights(action, s_ref, copy, at, w_refs, w_buf, sems):
    def run(source):
        for src, slot in source(s_ref, w_refs):
            where = w_buf.at[at] if slot is None else w_buf.at[at, slot]
            getattr(pltpu.make_async_copy(src, where, sems.at[at]), action)()

    main, other = copy
    if other is None:
        run(main)
        return

    @pl.when(s_ref[2] == 1)
    def _():
        run(main)

    @pl.when(s_ref[2] == 0)
    def _():
        run(other)


def out_kernel(n, copies, n_w, s_ref, glu, *refs):
    w_refs, outs, (acc, w_buf, sems) = refs[:n_w], refs[n_w:-3], refs[-3:]
    for k, copy in enumerate(copies):
        move_weights("start", s_ref, copy, k, w_refs, w_buf, sems)
    tokens, blk = glu.shape[2:]
    for k, copy in enumerate(copies):
        move_weights("wait", s_ref, copy, k, w_refs, w_buf, sems)
        part = jnp.dot(
            glu[s_ref[3] ^ k].reshape(n * tokens, blk),
            w_buf[k].reshape(blk, w_buf.shape[3]),
            preferred_element_type=F32,
        )
        if k == 0:
            acc[...] = part
        else:
            acc[...] += part
    for k, out in enumerate(outs):
        out[...] = acc[k * tokens : (k + 1) * tokens, :].astype(out.dtype)


def grad_kernel(n, jb, rl, blocks, copies, n_w, aliased, s_ref, own, *refs):
    received, refs = refs[: n - 1], refs[n - 1 :]
    (taps, silu, slope), refs = refs[:3], refs[3:]
    cots, refs = refs[:n], refs[n:]
    w_refs, refs = refs[:n_w], refs[n_w + aliased :]
    outs, (tap_grad, xs, dp, dh, cot_all, w_buf, sems, cot_sems) = refs[:n], refs[n:]
    b, tap_mask = s_ref[0], s_ref[1]
    step = pl.program_id(0)
    jz = s_ref[3] ^ (step * blocks.step + blocks.start)
    tokens, blk = silu.shape[2:]
    cols = tokens // rl
    total = n * rl

    def move_cots(action):
        for k in range(n):
            where = cot_all.at[pl.ds(k * tokens, tokens)]
            getattr(pltpu.make_async_copy(cots[k], where, cot_sems.at[k]), action)()

    @pl.when(step == 0)
    def _():
        move_cots("start")
        for at in range(len(copies)):
            move_weights("start", s_ref, copies[at], at, w_refs, w_buf, sems)

    place_rows(n, rl, b, xs, own, received)

    @pl.when(step == 0)
    def _():
        move_cots("wait")

    for at in range(len(copies)):
        @pl.when(step == at)
        def _():
            move_weights("wait", s_ref, copies[at], at, w_refs, w_buf, sems)

    d_glu = lax.dot_general(
        cot_all[...],
        w_buf[step].reshape(blk, w_buf.shape[3]),
        (((1,), (1,)), ((), ())),
        preferred_element_type=F32,
    ).reshape(n, tokens, blk)
    dp[0] = (d_glu * silu[0]).astype(BF16).astype(F32).reshape(n, rl, cols, blk)
    dp[1] = (d_glu * slope[0]).astype(BF16).astype(F32).reshape(n, rl, cols, blk)

    def fold(value):
        return jnp.sum(value.reshape(cols // 8, 8, value.shape[1]), axis=0)

    for vg in range(2):
        for lanes in lane_tiles(blk):
            w = taps[(vg * jb + jz) ^ tap_mask, :, lanes].astype(F32)
            acc = [None] * total
            sums = [None] * 10
            for r in range(total):
                row = dp[vg, lax.rem(r // rl - b + n, n), r % rl, :, lanes]
                seen = shifted(row)
                part = fold(row)
                sums[9] = part if sums[9] is None else sums[9] + part
                for i in range(3):
                    to = r - 1 + i
                    if not 0 <= to < total:
                        continue
                    x = xs[vg, to, :, lanes]
                    term = sum(w[3 * i + j : 3 * i + j + 1] * seen[2 - j] for j in range(3))
                    acc[to] = term if acc[to] is None else acc[to] + term
                    for j in range(3):
                        part = fold(x * seen[2 - j])
                        tap = 3 * i + j
                        sums[tap] = part if sums[tap] is None else sums[tap] + part
                for to in [r - 1] if r < total - 1 else [r - 1, r]:
                    if to >= 0:
                        rel = lax.rem(to // rl - b + n, n)
                        dh[rel, vg, to % rl, :, lanes] = acc[to].astype(BF16)
            tap_grad[vg, 0, :10, lanes] = jnp.concatenate(
                [jnp.sum(v, axis=0, keepdims=True) for v in sums], axis=0
            )
    for k in range(n):
        for vg in range(2):
            outs[k][vg, 0] = dh[k, vg]


def unpack_kernel(n, jb, blk, chunks, sums, s_ref, *refs):
    b = s_ref[0]
    if sums:
        (mine, theirs), refs = refs[:2], refs[2:]
        taps, bias, held = refs[-3:]
        refs = refs[:-3] + (held,)
        for half in range(n):
            part = jnp.where(b == half, mine[...], theirs[...])
            taps[:, half * blk : (half + 1) * blk] = part[:9]
            bias[half * blk : (half + 1) * blk] = part[9]
    ins, out, held = refs[:-2], refs[-2], refs[-1]
    for c, blocks in enumerate(chunks):
        for k in range(n):
            for at, kz in enumerate(blocks):
                held[lax.rem(b - k + n, n), :, s_ref[3] ^ kz] = ins[c * n + k][:, at, 0]
    for vg in range(2):
        for jz in range(jb):
            for t in range(n):
                start = ((vg * jb + jz) * n + t) * blk
                out[:, start : start + blk] = held[t, vg, jz]


def unit(hidden_in, tap_weights, tap_bias, w_out, cotangent):
    groups, shards, n = (lax.axis_size(a) for a in ("groups", "fsdp", "band"))
    images, rl, cols, chans = hidden_in.shape
    blk = w_out.shape[0]
    jb = shards // n
    feats = w_out.shape[1]
    tokens = rl * cols
    g, f, b = (lax.axis_index(a) for a in ("groups", "fsdp", "band"))
    fast = n == 2 and groups == 2 and shards % 4 == 0 and shards & (shards - 1) == 0 and blk % 32 == 0
    assert images == 1 and shards % n == 0

    tap_block = jnp.concatenate(
        [tap_weights, tap_bias[None], jnp.zeros((6, tap_bias.shape[0]), BF16)], axis=0
    )
    if fast:
        scalars = jnp.stack([b, f // 2 * 2 + 1 - b, jnp.where(f % 2 == b, 1, 0), f // n, g]).astype(jnp.int32)
    else:
        scalars = jnp.stack([b, 0 * f, 0 * f + 1, 0 * f, 0 * g]).astype(jnp.int32)

    vmem = pl.BlockSpec(memory_space=pltpu.VMEM)
    smem = pl.BlockSpec(memory_space=pltpu.SMEM)
    any_spec = pl.BlockSpec(memory_space=pl.ANY)
    part_shape = (2, jb, rl, cols, blk)
    packed = pl.pallas_call(
        functools.partial(pack_kernel, n, jb, blk),
        grid_spec=pltpu.PrefetchScalarGridSpec(
            num_scalar_prefetch=1,
            grid=(rl,),
            in_specs=[pl.BlockSpec((cols, chans), lambda i, s: (i, 0))],
            out_specs=[pl.BlockSpec((2, jb, 1, cols, blk), lambda i, s: (0, 0, i, 0, 0))] * n,
            scratch_shapes=[pltpu.VMEM((n, 2, jb, cols, blk), BF16)],
        ),
        out_shape=[jax.ShapeDtypeStruct(part_shape, BF16)] * n,
        name="pack",
    )(scalars, hidden_in.reshape(tokens, chans))

    if fast:
        every = ("groups", "fsdp", "band")
        zr = jb

        def across(x, flip):
            pairs = [
                (s * n + t, (s ^ flip) * n + t)
                for s in range(shards) for t in range(n) if flip == 1 or s % 2 == t
            ]
            return lax.ppermute(x, ("fsdp", "band"), pairs)

        def other_group(x):
            size = shards * n
            pairs = [
                (p * size + s * n + t, (1 - p) * size + s * n + t)
                for p in range(2) for s in range(shards) for t in range(n) if s % 2 == t
            ]
            return lax.ppermute(x, every, pairs)

        mine = {0: lax.dynamic_slice_in_dim(w_out, g * (blk // 2), blk // 2, 0)}
        order = []
        bit = zr // 2
        while bit:
            order.append(bit)
            bit //= 2
        for bit in order:
            for k in list(mine):
                mine[k ^ bit] = across(mine[k], 2 * bit)
        w_parts = []
        for k in range(zr):
            if k == 0:
                pair = [w_out, across(w_out, 1)]
                w_parts.append(([w.reshape(2, blk // 2, feats) for w in pair], False))
            else:
                a, y = mine[k], other_group(mine[k])
                w_parts.append(([a, y, across(a, 1), across(y, 1)], True))
        parts = 2
    else:
        w_all = lax.all_gather(w_out, "fsdp", axis=0, tiled=True).reshape(jb, n, 1, blk, feats)
        w_args = [lax.dynamic_index_in_dim(w_all, b, 1, keepdims=False)]
        copies = [(lambda s, w, k=k: [(w[0].at[k], None)], None) for k in range(jb)]
        parts = 1

    if fast:
        tap_own = lax.dynamic_slice_in_dim(tap_block, b * blk, blk, 1)
        tap_pair = jnp.stack([tap_own, across(tap_own, 1)])
        tap_all = [tap_pair]
        for k in range(1, zr):
            pairs = [
                (s * n + t, (s ^ 2 * k) * n + t) for s in range(shards) for t in range(n) if s % 2 != t
            ]
            tap_all.append(lax.ppermute(tap_pair, ("fsdp", "band"), pairs))
        tap_all = jnp.concatenate(tap_all, axis=0)
        tap_all = jnp.where(f % 2 == b, across(tap_all, 1), tap_all)
    else:
        tap_all = lax.all_gather(tap_block, "fsdp", axis=1, tiled=True)
        tap_all = tap_all.reshape(16, 2 * jb, n, blk)
        tap_all = lax.dynamic_index_in_dim(tap_all, b, 2, keepdims=False).transpose(1, 0, 2)

    def turn(x, k):
        return lax.ppermute(x, "band", [(i, (i + k) % n) for i in range(n)])

    hid_in = [turn(packed[k], k) for k in range(1, n)]
    cots = [cotangent] + [turn(cotangent, n - k) for k in range(1, n)]
    cots = [c.reshape(tokens, feats) for c in cots]

    part_spec = pl.BlockSpec((2, 1, rl, cols, blk), lambda j, s: (0, j, 0, 0, 0))
    tap_spec = pl.BlockSpec((2 * jb, 16, blk), lambda j, s: (0, 0, 0))
    act_spec = pl.BlockSpec((1, n, tokens, blk), lambda j, s: (j, 0, 0, 0))
    act_shape = (jb, n, tokens, blk)
    glu, silu, slope = pl.pallas_call(
        functools.partial(conv_kernel, n, jb, rl),
        grid_spec=pltpu.PrefetchScalarGridSpec(
            num_scalar_prefetch=1,
            grid=(jb,),
            in_specs=[part_spec] * n + [tap_spec],
            out_specs=[act_spec] * 3,
            scratch_shapes=[
                pltpu.VMEM((2, n * rl, cols, blk), F32),
                pltpu.VMEM((n * rl, cols, LANES), F32),
            ],
        ),
        out_shape=[
            jax.ShapeDtypeStruct(act_shape, BF16),
            jax.ShapeDtypeStruct(act_shape, F32),
            jax.ShapeDtypeStruct(act_shape, F32),
        ],
        name="conv",
    )(scalars, packed[0], *hid_in, tap_all)

    chunks = CHUNKS if fast and jb == 4 else [range(jb)]

    def weights_of(blocks):
        if not fast:
            return w_args, copies
        args, moves = [], []
        for k in blocks:
            arrays, halves = w_parts[k]
            base = len(args)
            args += arrays
            if halves:
                moves.append((
                    lambda s, w, i=base: [(w[i], s[4]), (w[i + 1], 1 - s[4])],
                    lambda s, w, i=base + 2: [(w[i], s[4]), (w[i + 1], 1 - s[4])],
                ))
            else:
                moves.append((
                    lambda s, w, i=base: [(w[i], None)],
                    lambda s, w, i=base + 1: [(w[i], None)],
                ))
        return args, moves

    args, moves = weights_of(range(jb))
    partial = pl.pallas_call(
        functools.partial(out_kernel, n, moves, len(args)),
        in_specs=[smem, vmem] + [any_spec] * len(args),
        out_specs=[vmem] * n,
        out_shape=[jax.ShapeDtypeStruct((tokens, feats), F32 if k == 0 else BF16) for k in range(n)],
        scratch_shapes=[
            pltpu.VMEM((n * tokens, feats), F32),
            pltpu.VMEM((jb, parts, blk // parts, feats), BF16),
            pltpu.SemaphoreType.DMA((jb,)),
        ],
        name="project",
    )(scalars, glu, *args)
    partial = [p.reshape(cotangent.shape) for p in partial]
    others = [turn(partial[k], k) for k in range(1, n)]
    block_out = partial[0]
    for other in others:
        block_out = block_out + other.astype(F32)
    block_out = block_out.astype(BF16)

    tap_grad, d_parts = None, []
    for blocks in chunks:
        args, moves = weights_of(blocks)
        at = lambda j, s, c=blocks: s[3] ^ (j * c.step + c.start)
        part_at = pl.BlockSpec((2, 1, rl, cols, blk), lambda j, s, at=at: (0, at(j, s), 0, 0, 0))
        act_at = pl.BlockSpec((1, n, tokens, blk), lambda j, s, at=at: (at(j, s), 0, 0, 0))
        aliased = 0 if tap_grad is None else 1
        outs = pl.pallas_call(
            functools.partial(grad_kernel, n, jb, rl, blocks, moves, len(args), aliased),
            grid_spec=pltpu.PrefetchScalarGridSpec(
                num_scalar_prefetch=1,
                grid=(len(blocks),),
                in_specs=[part_at] * n + [tap_spec, act_at, act_at] + [any_spec] * (n + len(args) + aliased),
                out_specs=[part_spec] * n
                + [pl.BlockSpec((2, 1, 16, blk), lambda j, s, at=at: (0, at(j, s), 0, 0))],
                scratch_shapes=[
                    pltpu.VMEM((2, n * rl, cols, blk), F32),
                    pltpu.VMEM((2, n, rl, cols, blk), F32),
                    pltpu.VMEM((n, 2, rl, cols, blk), BF16),
                    pltpu.VMEM((n * tokens, feats), BF16),
                    pltpu.VMEM((len(blocks), parts, blk // parts, feats), BF16),
                    pltpu.SemaphoreType.DMA((len(blocks),)),
                    pltpu.SemaphoreType.DMA((n,)),
                ],
            ),
            out_shape=[jax.ShapeDtypeStruct((2, len(blocks), rl, cols, blk), BF16)] * n
            + [jax.ShapeDtypeStruct((2, jb, 16, blk), F32)],
            input_output_aliases={4 + 2 * n + len(args): n} if aliased else {},
        )(
            scalars, packed[0], *hid_in, tap_all, silu, slope, *cots, *args,
            *([tap_grad] if aliased else []),
        )
        tap_grad = outs[n]
        d_parts += [outs[0]] + [turn(outs[k], k) for k in range(1, n)]
    tap_grad = tap_grad.reshape(2 * jb, 16, blk)
    if fast:
        pieces = lax.all_to_all(tap_grad, "fsdp", 0, 0, tiled=True)
        mine_sum = jnp.sum(pieces, axis=0)
        sums = [mine_sum, turn(mine_sum, 1)]
    else:
        sums = []
        spread = jnp.where(
            (jnp.arange(n) == b)[None, None, :, None], tap_grad.transpose(1, 0, 2)[:, :, None, :], 0.0
        ).reshape(16, chans)
        share = lax.psum(spread, "band")
        share = lax.psum_scatter(share, "fsdp", scatter_dimension=1, tiled=True)

    whole = lambda shape: pl.BlockSpec(shape, lambda i, s: (0, 0))
    row_specs = [pl.BlockSpec((2, p.shape[1], 1, cols, blk), lambda i, s: (0, 0, i, 0, 0)) for p in d_parts]
    outs = pl.pallas_call(
        functools.partial(unpack_kernel, n, jb, blk, chunks, len(sums)),
        grid_spec=pltpu.PrefetchScalarGridSpec(
            num_scalar_prefetch=1,
            grid=(rl,),
            in_specs=[whole((16, blk))] * len(sums) + row_specs,
            out_specs=[pl.BlockSpec((cols, chans), lambda i, s: (i, 0))]
            + ([whole((9, n * blk)), pl.BlockSpec((n * blk,), lambda i, s: (0,))] if sums else []),
            scratch_shapes=[pltpu.VMEM((n, 2, jb, cols, blk), BF16)],
        ),
        out_shape=[jax.ShapeDtypeStruct((tokens, chans), BF16)]
        + ([jax.ShapeDtypeStruct(shape, F32) for shape in ((9, n * blk), (n * blk,))] if sums else []),
        name="unpack",
    )(scalars, *sums, *d_parts)
    d_hidden = outs[0]
    d_taps, d_bias = (outs[1], outs[2]) if sums else (share[:9], share[9])
    return (
        block_out,
        d_hidden.reshape(hidden_in.shape),
        d_taps,
        d_bias,
    )


CHUNKS = [range(0, 2), range(2, 4)]


def solution(mesh):
    placed = (
        P(("groups", "fsdp"), "band", None, None),
        P(None, "fsdp"),
        P("fsdp"),
        P("fsdp", None),
        P(("groups", "fsdp"), "band", None, None),
    )
    return jax.shard_map(
        unit,
        mesh=mesh,
        in_specs=placed,
        out_specs=(
            P(("groups", "fsdp"), "band", None, None),
            P(("groups", "fsdp"), "band", None, None),
            P("groups", "fsdp"),
            P(("groups", "fsdp")),
        ),
        check_vma=False,
    )
```

```python
import functools

import jax
import jax.numpy as jnp
from jax import lax
from jax.experimental import pallas as pl
from jax.experimental.pallas import tpu as pltpu
from jax.sharding import PartitionSpec as P


F32 = jnp.float32
BF16 = jnp.bfloat16
LANES = 128


def up(value, step):
    return -(-value // step) * step


def pack_kernel(n, jb, blk, s_ref, x_ref, *refs):
    outs, held = refs[:-1], refs[-1]
    b = s_ref[0]
    chans = x_ref.shape[1]
    for vg in range(2):
        for jz in range(jb):
            for t in range(n):
                start = ((vg * jb + jz) * n + t) * blk
                low = start // LANES * LANES
                high = min(up(start + blk, LANES), chans)
                wide = x_ref[:, low:high].astype(F32)
                if start != low:
                    wide = pltpu.roll(wide, high - low - (start - low), 1)
                held[lax.rem(t - b + n, n), vg, jz] = wide[:, :blk].astype(BF16)
    for k in range(n):
        outs[k][:, :, 0] = held[k]


def place_rows(n, rl, b, xs, own, received):
    for vg in range(2):
        for i in range(rl):
            xs[vg, b * rl + i] = own[vg, 0, i].astype(F32)
            for k in range(1, n):
                src = lax.rem(b - k + n, n)
                xs[vg, src * rl + i] = received[k - 1][vg, 0, i].astype(F32)


def shifted(row):
    cols = row.shape[0]
    at = lax.broadcasted_iota(jnp.int32, row.shape, 0)
    prev = jnp.where(at == 0, 0.0, pltpu.roll(row, 1, 0))
    nxt = jnp.where(at == cols - 1, 0.0, pltpu.roll(row, cols - 1, 0))
    return prev, row, nxt


def lane_tiles(blk):
    return [pl.ds(low, min(LANES, blk - low)) for low in range(0, blk, LANES)]


def conv_kernel(n, jb, rl, s_ref, own, *refs):
    received, (taps, glu, silu, slope, xs, pres) = refs[: n - 1], refs[n - 1 :]
    b, tap_mask = s_ref[0], s_ref[1]
    jz = pl.program_id(0)
    place_rows(n, rl, b, xs, own, received)
    total = n * rl
    cols, blk = own.shape[3:]
    for lanes in lane_tiles(blk):
        for vg in range(2):
            w = taps[(vg * jb + jz) ^ tap_mask, :, lanes].astype(F32)
            acc = [None] * total
            for r in range(total):
                parts = shifted(xs[vg, r, :, lanes])
                for i in range(3):
                    to = r + 1 - i
                    if 0 <= to < total:
                        term = sum(w[3 * i + j : 3 * i + j + 1] * parts[j] for j in range(3))
                        acc[to] = term + w[9:10] if acc[to] is None else acc[to] + term
                done = [r - 1] if r < total - 1 else [r - 1, r]
                for at in done:
                    if at < 0:
                        continue
                    if vg == 0:
                        pres[at] = acc[at] if acc[at].shape[1] == LANES else jnp.pad(
                            acc[at], ((0, 0), (0, LANES - acc[at].shape[1]))
                        )
                        continue
                    values, gate = pres[at][:, : acc[at].shape[1]], acc[at]
                    rel = lax.rem(at // rl - b + n, n)
                    sigma = jax.nn.sigmoid(gate)
                    act = gate * sigma
                    spot = pl.ds(at % rl * cols, cols)
                    glu[0, rel, spot, lanes] = (values * act).astype(BF16)
                    silu[0, rel, spot, lanes] = act
                    slope[0, rel, spot, lanes] = values * (sigma * (1.0 + gate * (1.0 - sigma)))


def move_weights(action, s_ref, copy, at, w_refs, w_buf, sems):
    def run(source):
        for src, slot in source(s_ref, w_refs):
            where = w_buf.at[at] if slot is None else w_buf.at[at, slot]
            getattr(pltpu.make_async_copy(src, where, sems.at[at]), action)()

    main, other = copy
    if other is None:
        run(main)
        return

    @pl.when(s_ref[2] == 1)
    def _():
        run(main)

    @pl.when(s_ref[2] == 0)
    def _():
        run(other)


def out_kernel(n, copies, n_w, s_ref, glu, *refs):
    w_refs, outs, (acc, pair, w_buf, sems) = refs[:n_w], refs[n_w:-4], refs[-4:]
    for k, copy in enumerate(copies):
        move_weights("start", s_ref, copy, k, w_refs, w_buf, sems)
    tokens, blk = glu.shape[2:]
    width = pair.shape[1] // blk
    for low in range(0, len(copies), width):
        for at in range(width):
            pair[:, at * blk : (at + 1) * blk] = glu[s_ref[3] ^ (low + at)].reshape(n * tokens, blk)
        for at in range(width):
            move_weights("wait", s_ref, copies[low + at], low + at, w_refs, w_buf, sems)
        part = jnp.dot(
            pair[...],
            w_buf[low : low + width].reshape(width * blk, w_buf.shape[3]),
            preferred_element_type=F32,
        )
        if low == 0:
            acc[...] = part
        else:
            acc[...] += part
    for k, out in enumerate(outs):
        out[...] = acc[k * tokens : (k + 1) * tokens, :].astype(out.dtype)


def grad_kernel(n, jb, rl, blocks, copies, n_w, aliased, s_ref, own, *refs):
    received, refs = refs[: n - 1], refs[n - 1 :]
    (taps, silu, slope), refs = refs[:3], refs[3:]
    cots, refs = refs[:n], refs[n:]
    w_refs, refs = refs[:n_w], refs[n_w + aliased :]
    outs, (tap_grad, xs, dp, dh, cot_all, w_buf, sems, cot_sems) = refs[:n], refs[n:]
    b, tap_mask = s_ref[0], s_ref[1]
    step = pl.program_id(0)
    jz = s_ref[3] ^ (step * blocks.step + blocks.start)
    tokens, blk = silu.shape[2:]
    cols = tokens // rl
    total = n * rl

    def move_cots(action):
        for k in range(n):
            where = cot_all.at[pl.ds(k * tokens, tokens)]
            getattr(pltpu.make_async_copy(cots[k], where, cot_sems.at[k]), action)()

    @pl.when(step == 0)
    def _():
        move_weights("start", s_ref, copies[0], 0, w_refs, w_buf, sems)
        move_cots("start")
        for at in range(1, len(copies)):
            move_weights("start", s_ref, copies[at], at, w_refs, w_buf, sems)

    place_rows(n, rl, b, xs, own, received)

    @pl.when(step == 0)
    def _():
        move_cots("wait")

    for at in range(len(copies)):
        @pl.when(step == at)
        def _():
            move_weights("wait", s_ref, copies[at], at, w_refs, w_buf, sems)

    d_glu = lax.dot_general(
        cot_all[...],
        w_buf[step].reshape(blk, w_buf.shape[3]),
        (((1,), (1,)), ((), ())),
        preferred_element_type=F32,
    ).reshape(n, tokens, blk)
    dp[0] = (d_glu * silu[0]).astype(BF16).astype(F32).reshape(n, rl, cols, blk)
    dp[1] = (d_glu * slope[0]).astype(BF16).astype(F32).reshape(n, rl, cols, blk)

    def fold(value):
        return jnp.sum(value.reshape(cols // 8, 8, value.shape[1]), axis=0)

    for vg in range(2):
        for lanes in lane_tiles(blk):
            w = taps[(vg * jb + jz) ^ tap_mask, :, lanes].astype(F32)
            acc = [None] * total
            sums = [None] * 10
            for r in range(total):
                row = dp[vg, lax.rem(r // rl - b + n, n), r % rl, :, lanes]
                seen = shifted(row)
                part = fold(row)
                sums[9] = part if sums[9] is None else sums[9] + part
                for i in range(3):
                    to = r - 1 + i
                    if not 0 <= to < total:
                        continue
                    x = xs[vg, to, :, lanes]
                    term = sum(w[3 * i + j : 3 * i + j + 1] * seen[2 - j] for j in range(3))
                    acc[to] = term if acc[to] is None else acc[to] + term
                    for j in range(3):
                        part = fold(x * seen[2 - j])
                        tap = 3 * i + j
                        sums[tap] = part if sums[tap] is None else sums[tap] + part
                for to in [r - 1] if r < total - 1 else [r - 1, r]:
                    if to >= 0:
                        rel = lax.rem(to // rl - b + n, n)
                        dh[rel, vg, to % rl, :, lanes] = acc[to].astype(BF16)
            tap_grad[vg, 0, :10, lanes] = jnp.concatenate(
                [jnp.sum(v, axis=0, keepdims=True) for v in sums], axis=0
            )
    for k in range(n):
        for vg in range(2):
            outs[k][vg, 0] = dh[k, vg]


def unpack_kernel(n, jb, blk, chunks, sums, s_ref, *refs):
    b = s_ref[0]
    if sums:
        (mine, theirs), refs = refs[:2], refs[2:]
        taps, bias, held = refs[-3:]
        refs = refs[:-3] + (held,)
        for half in range(n):
            part = jnp.where(b == half, mine[...], theirs[...])
            taps[:, half * blk : (half + 1) * blk] = part[:9]
            bias[half * blk : (half + 1) * blk] = part[9]
    ins, out, held = refs[:-2], refs[-2], refs[-1]
    for c, blocks in enumerate(chunks):
        for k in range(n):
            for at, kz in enumerate(blocks):
                held[lax.rem(b - k + n, n), :, s_ref[3] ^ kz] = ins[c * n + k][:, at, 0]
    for vg in range(2):
        for jz in range(jb):
            for t in range(n):
                start = ((vg * jb + jz) * n + t) * blk
                out[:, start : start + blk] = held[t, vg, jz]


def unit(hidden_in, tap_weights, tap_bias, w_out, cotangent):
    groups, shards, n = (lax.axis_size(a) for a in ("groups", "fsdp", "band"))
    images, rl, cols, chans = hidden_in.shape
    blk = w_out.shape[0]
    jb = shards // n
    feats = w_out.shape[1]
    tokens = rl * cols
    g, f, b = (lax.axis_index(a) for a in ("groups", "fsdp", "band"))
    fast = n == 2 and groups == 2 and shards % 4 == 0 and shards & (shards - 1) == 0 and blk % 32 == 0
    assert images == 1 and shards % n == 0

    tap_block = jnp.concatenate(
        [tap_weights, tap_bias[None], jnp.zeros((6, tap_bias.shape[0]), BF16)], axis=0
    )
    if fast:
        scalars = jnp.stack([b, f // 2 * 2 + 1 - b, jnp.where(f % 2 == b, 1, 0), f // n, g]).astype(jnp.int32)
    else:
        scalars = jnp.stack([b, 0 * f, 0 * f + 1, 0 * f, 0 * g]).astype(jnp.int32)

    vmem = pl.BlockSpec(memory_space=pltpu.VMEM)
    smem = pl.BlockSpec(memory_space=pltpu.SMEM)
    any_spec = pl.BlockSpec(memory_space=pl.ANY)
    part_shape = (2, jb, rl, cols, blk)
    packed = pl.pallas_call(
        functools.partial(pack_kernel, n, jb, blk),
        grid_spec=pltpu.PrefetchScalarGridSpec(
            num_scalar_prefetch=1,
            grid=(rl,),
            in_specs=[pl.BlockSpec((cols, chans), lambda i, s: (i, 0))],
            out_specs=[pl.BlockSpec((2, jb, 1, cols, blk), lambda i, s: (0, 0, i, 0, 0))] * n,
            scratch_shapes=[pltpu.VMEM((n, 2, jb, cols, blk), BF16)],
        ),
        out_shape=[jax.ShapeDtypeStruct(part_shape, BF16)] * n,
        name="pack",
    )(scalars, hidden_in.reshape(tokens, chans))

    if fast:
        every = ("groups", "fsdp", "band")
        zr = jb

        def across(x, flip):
            pairs = [
                (s * n + t, (s ^ flip) * n + t)
                for s in range(shards) for t in range(n) if flip == 1 or s % 2 == t
            ]
            return lax.ppermute(x, ("fsdp", "band"), pairs)

        def other_group(x):
            size = shards * n
            pairs = [
                (p * size + s * n + t, (1 - p) * size + s * n + t)
                for p in range(2) for s in range(shards) for t in range(n) if s % 2 == t
            ]
            return lax.ppermute(x, every, pairs)

        mine = {0: lax.dynamic_slice_in_dim(w_out, g * (blk // 2), blk // 2, 0)}
        order = []
        bit = zr // 2
        while bit:
            order.append(bit)
            bit //= 2
        for bit in order:
            for k in list(mine):
                mine[k ^ bit] = across(mine[k], 2 * bit)
        w_parts = []
        for k in range(zr):
            if k == 0:
                pair = [w_out, across(w_out, 1)]
                w_parts.append(([w.reshape(2, blk // 2, feats) for w in pair], False))
            else:
                a, y = mine[k], other_group(mine[k])
                w_parts.append(([a, y, across(a, 1), across(y, 1)], True))
        parts = 2
    else:
        w_all = lax.all_gather(w_out, "fsdp", axis=0, tiled=True).reshape(jb, n, 1, blk, feats)
        w_args = [lax.dynamic_index_in_dim(w_all, b, 1, keepdims=False)]
        copies = [(lambda s, w, k=k: [(w[0].at[k], None)], None) for k in range(jb)]
        parts = 1

    if fast:
        tap_own = lax.dynamic_slice_in_dim(tap_block, b * blk, blk, 1)
        tap_pair = jnp.stack([tap_own, across(tap_own, 1)])
        tap_all = [tap_pair]
        for k in range(1, zr):
            pairs = [
                (s * n + t, (s ^ 2 * k) * n + t) for s in range(shards) for t in range(n) if s % 2 != t
            ]
            tap_all.append(lax.ppermute(tap_pair, ("fsdp", "band"), pairs))
        tap_all = jnp.concatenate(tap_all, axis=0)
        tap_all = jnp.where(f % 2 == b, across(tap_all, 1), tap_all)
    else:
        tap_all = lax.all_gather(tap_block, "fsdp", axis=1, tiled=True)
        tap_all = tap_all.reshape(16, 2 * jb, n, blk)
        tap_all = lax.dynamic_index_in_dim(tap_all, b, 2, keepdims=False).transpose(1, 0, 2)

    def turn(x, k):
        return lax.ppermute(x, "band", [(i, (i + k) % n) for i in range(n)])

    hid_in = [turn(packed[k], k) for k in range(1, n)]
    cots = [cotangent] + [turn(cotangent, n - k) for k in range(1, n)]
    cots = [c.reshape(tokens, feats) for c in cots]

    part_spec = pl.BlockSpec((2, 1, rl, cols, blk), lambda j, s: (0, j, 0, 0, 0))
    tap_spec = pl.BlockSpec((2 * jb, 16, blk), lambda j, s: (0, 0, 0))
    act_spec = pl.BlockSpec((1, n, tokens, blk), lambda j, s: (j, 0, 0, 0))
    act_shape = (jb, n, tokens, blk)
    glu, silu, slope = pl.pallas_call(
        functools.partial(conv_kernel, n, jb, rl),
        grid_spec=pltpu.PrefetchScalarGridSpec(
            num_scalar_prefetch=1,
            grid=(jb,),
            in_specs=[part_spec] * n + [tap_spec],
            out_specs=[act_spec] * 3,
            scratch_shapes=[
                pltpu.VMEM((2, n * rl, cols, blk), F32),
                pltpu.VMEM((n * rl, cols, LANES), F32),
            ],
        ),
        out_shape=[
            jax.ShapeDtypeStruct(act_shape, BF16),
            jax.ShapeDtypeStruct(act_shape, F32),
            jax.ShapeDtypeStruct(act_shape, F32),
        ],
        name="conv",
    )(scalars, packed[0], *hid_in, tap_all)

    chunks = CHUNKS if fast and jb == 4 else [range(jb)]

    def weights_of(blocks):
        if not fast:
            return w_args, copies
        args, moves = [], []
        for k in blocks:
            arrays, halves = w_parts[k]
            base = len(args)
            args += arrays
            if halves:
                moves.append((
                    lambda s, w, i=base: [(w[i], s[4]), (w[i + 1], 1 - s[4])],
                    lambda s, w, i=base + 2: [(w[i], s[4]), (w[i + 1], 1 - s[4])],
                ))
            else:
                moves.append((
                    lambda s, w, i=base: [(w[i], None)],
                    lambda s, w, i=base + 1: [(w[i], None)],
                ))
        return args, moves

    args, moves = weights_of(range(jb))
    partial = pl.pallas_call(
        functools.partial(out_kernel, n, moves, len(args)),
        in_specs=[smem, vmem] + [any_spec] * len(args),
        out_specs=[vmem] * n,
        out_shape=[jax.ShapeDtypeStruct((tokens, feats), F32 if k == 0 else BF16) for k in range(n)],
        scratch_shapes=[
            pltpu.VMEM((n * tokens, feats), F32),
            pltpu.VMEM((n * tokens, 2 * blk if fast else blk), BF16),
            pltpu.VMEM((jb, parts, blk // parts, feats), BF16),
            pltpu.SemaphoreType.DMA((jb,)),
        ],
        name="project",
    )(scalars, glu, *args)
    partial = [p.reshape(cotangent.shape) for p in partial]
    others = [turn(partial[k], k) for k in range(1, n)]
    block_out = partial[0]
    for other in others:
        block_out = block_out + other.astype(F32)
    block_out = block_out.astype(BF16)

    tap_grad, d_parts = None, []
    for blocks in chunks:
        args, moves = weights_of(blocks)
        at = lambda j, s, c=blocks: s[3] ^ (j * c.step + c.start)
        part_at = pl.BlockSpec((2, 1, rl, cols, blk), lambda j, s, at=at: (0, at(j, s), 0, 0, 0))
        act_at = pl.BlockSpec((1, n, tokens, blk), lambda j, s, at=at: (at(j, s), 0, 0, 0))
        aliased = 0 if tap_grad is None else 1
        outs = pl.pallas_call(
            functools.partial(grad_kernel, n, jb, rl, blocks, moves, len(args), aliased),
            grid_spec=pltpu.PrefetchScalarGridSpec(
                num_scalar_prefetch=1,
                grid=(len(blocks),),
                in_specs=[part_at] * n + [tap_spec, act_at, act_at] + [any_spec] * (n + len(args) + aliased),
                out_specs=[part_spec] * n
                + [pl.BlockSpec((2, 1, 16, blk), lambda j, s, at=at: (0, at(j, s), 0, 0))],
                scratch_shapes=[
                    pltpu.VMEM((2, n * rl, cols, blk), F32),
                    pltpu.VMEM((2, n, rl, cols, blk), F32),
                    pltpu.VMEM((n, 2, rl, cols, blk), BF16),
                    pltpu.VMEM((n * tokens, feats), BF16),
                    pltpu.VMEM((len(blocks), parts, blk // parts, feats), BF16),
                    pltpu.SemaphoreType.DMA((len(blocks),)),
                    pltpu.SemaphoreType.DMA((n,)),
                ],
            ),
            out_shape=[jax.ShapeDtypeStruct((2, len(blocks), rl, cols, blk), BF16)] * n
            + [jax.ShapeDtypeStruct((2, jb, 16, blk), F32)],
            input_output_aliases={4 + 2 * n + len(args): n} if aliased else {},
        )(
            scalars, packed[0], *hid_in, tap_all, silu, slope, *cots, *args,
            *([tap_grad] if aliased else []),
        )
        tap_grad = outs[n]
        d_parts += [outs[0]] + [turn(outs[k], k) for k in range(1, n)]
    tap_grad = tap_grad.reshape(2 * jb, 16, blk)
    if fast:
        pieces = lax.all_to_all(tap_grad, "fsdp", 0, 0, tiled=True)
        mine_sum = jnp.sum(pieces, axis=0)
        sums = [mine_sum, turn(mine_sum, 1)]
    else:
        sums = []
        spread = jnp.where(
            (jnp.arange(n) == b)[None, None, :, None], tap_grad.transpose(1, 0, 2)[:, :, None, :], 0.0
        ).reshape(16, chans)
        share = lax.psum(spread, "band")
        share = lax.psum_scatter(share, "fsdp", scatter_dimension=1, tiled=True)

    whole = lambda shape: pl.BlockSpec(shape, lambda i, s: (0, 0))
    row_specs = [pl.BlockSpec((2, p.shape[1], 1, cols, blk), lambda i, s: (0, 0, i, 0, 0)) for p in d_parts]
    outs = pl.pallas_call(
        functools.partial(unpack_kernel, n, jb, blk, chunks, len(sums)),
        grid_spec=pltpu.PrefetchScalarGridSpec(
            num_scalar_prefetch=1,
            grid=(rl,),
            in_specs=[whole((16, blk))] * len(sums) + row_specs,
            out_specs=[pl.BlockSpec((cols, chans), lambda i, s: (i, 0))]
            + ([whole((9, n * blk)), pl.BlockSpec((n * blk,), lambda i, s: (0,))] if sums else []),
            scratch_shapes=[pltpu.VMEM((n, 2, jb, cols, blk), BF16)],
        ),
        out_shape=[jax.ShapeDtypeStruct((tokens, chans), BF16)]
        + ([jax.ShapeDtypeStruct(shape, F32) for shape in ((9, n * blk), (n * blk,))] if sums else []),
        name="unpack",
    )(scalars, *sums, *d_parts)
    d_hidden = outs[0]
    d_taps, d_bias = (outs[1], outs[2]) if sums else (share[:9], share[9])
    return (
        block_out,
        d_hidden.reshape(hidden_in.shape),
        d_taps,
        d_bias,
    )


CHUNKS = [range(0, 2), range(2, 4)]


def solution(mesh):
    placed = (
        P(("groups", "fsdp"), "band", None, None),
        P(None, "fsdp"),
        P("fsdp"),
        P("fsdp", None),
        P(("groups", "fsdp"), "band", None, None),
    )
    return jax.shard_map(
        unit,
        mesh=mesh,
        in_specs=placed,
        out_specs=(
            P(("groups", "fsdp"), "band", None, None),
            P(("groups", "fsdp"), "band", None, None),
            P("groups", "fsdp"),
            P(("groups", "fsdp")),
        ),
        check_vma=False,
    )
```
